32 devices in a mesh: ctx: 8 (over y, x, core), exp: 4 (over z).
Axes of the slice: x: 2, y: 2, z: 4, core: 2. Of those that a mesh axis runs over, the one named last changes fastest.
Arguments:
- query: bfloat16 [1024, 4096], P('ctx', 'exp'), may hold values from -8 to 8
- keys_values: bfloat16 [2, 1024, 1024], P(None, 'ctx', 'exp'), may hold values from -8 to 8
- cache: bfloat16 [2, 2048, 1024], P(None, 'ctx', 'exp'), may hold values from -8 to 8
- residual: bfloat16 [1024, 4096], P(('ctx', 'exp')), may hold values from -6 to 6
- out_proj: bfloat16 [4096, 4096], P('exp'), may hold values from -0.09375 to 0.09375
- norm_gain: float32 [4096], replicated, may hold values from 0.1 to 1.9
- router: bfloat16 [4096, 4], replicated, may hold values from -0.09375 to 0.09375
- expert_ids: int32 [1024, 2], P(('ctx', 'exp')), may hold values from 0 to 3, all different within a row; in each aligned block of 32 rows (0 to 31, 32 to 63, ...) at most 32 rows name the same one
- w_gate: bfloat16 [4, 4096, 8192], P('exp', None, 'ctx'), may hold values from -0.09375 to 0.09375
- w_up: bfloat16 [4, 4096, 8192], P('exp', None, 'ctx'), may hold values from -0.09375 to 0.09375
- w_down: bfloat16 [4, 8192, 4096], P('exp', 'ctx'), may hold values from -0.0625 to 0.0625
- cotangent: bfloat16 [1024, 4096], P(('ctx', 'exp')), may hold values from -6 to 6
Outputs:
- layer_out: bfloat16 [1024, 4096], P(('ctx', 'exp'))
- grad_down: float32 [4, 8192, 4096], P('exp', 'ctx')
The draws below stay inside these ranges and needn't reach their ends.
Inputs may be any that keep to these rules, and one draw needn't show every extreme that they name: `expert_ids`: each row names two different experts. Within each aligned block of 32 rows no expert is named by more than 32 rows.
All inputs are finite; a program needn't handle non-finite values.
Results may differ from the reference program's by a relative error of at most 0.012.
Values may be sent and summed in bfloat16 or wider, within the bound.
No kernel may reach another device: no remote copies, remote signals or barrier semaphores. Data moves between devices by JAX's collectives and lax.ppermute only.
A program may use at most 128 MiB of HBM per device.

```python
import math
import jax
import jax.numpy as jnp
import numpy as np
from jax import lax

D = 4096
QUERY_HEADS = 32
KEY_VALUE_HEADS = 8
HEAD_SIZE = 128
FF = 8192
WINDOW = 4096
EXPERTS = 4
NEW_TOKENS = 1024
CACHED_TOKENS = 2048
ROWS_DEV = 32
CAP = 32
N_CTX = 8
N_EXP = 4


def drawn_pair(key):
    base = jax.random.fold_in(key, 101)
    key_query, key_index_pairs = jax.random.split(base, 2)
    queries = jax.random.normal(key_query, (NEW_TOKENS, QUERY_HEADS * HEAD_SIZE), jnp.float32)
    index_pairs = jax.random.normal(key_index_pairs, (2, NEW_TOKENS, KEY_VALUE_HEADS * HEAD_SIZE), jnp.float32)
    return (jnp.clip(queries, -8.0, 8.0), jnp.clip(index_pairs, -8.0, 8.0))


def draw_query(key, part):
    return drawn_pair(key)[0].astype(jnp.bfloat16)


def draw_keys_values(key, part):
    return drawn_pair(key)[1].astype(jnp.bfloat16)


def shard_levels(rng, dims, cuts, least, high):
    loudness, own = 1.0, jax.random.fold_in(rng, 6)
    for axis_at, shards_of in cuts:
        steps = jnp.exp(jax.random.uniform(jax.random.fold_in(own, axis_at), (shards_of,), jnp.float32, least / len(cuts), high / len(cuts)))
        loudness = loudness * jnp.repeat(steps, dims[axis_at] // shards_of).reshape([-1 if axis == axis_at else 1 for axis in range(len(dims))])
    return loudness


def routed_block(stream_key, own, number, rows, amount, top, reach, slope):
    order = jax.random.permutation(stream_key, amount)
    crowded, ordinary = load_shares(amount, rows * top, reach, slope, True), load_shares(amount, rows * top, reach, slope, False)
    places = jnp.arange(amount)

    def named(sizes, turn):
        used = int((sizes > 0).sum())
        fixed = max(1, used // 4)
        moved = fixed + (places - fixed + turn * (used - fixed)) % max(1, amount - fixed)
        return jnp.zeros((amount,), jnp.int32).at[order[jnp.where(places < fixed, places, moved)]].set(jnp.asarray(sizes, jnp.int32))

    sizes = jnp.where(number % 4 == 0, named(crowded, number // 4), named(ordinary, number - number // 4 - 1))
    mixed = jax.random.permutation(jax.random.fold_in(own, 3), amount)
    source_of, sink = mixed[0:amount // 2 * 2:2], mixed[1:amount // 2 * 2:2]
    margin = jnp.minimum(sizes[source_of] - 1, reach - sizes[sink]) // 2
    margin = jnp.where((source_of == order[0]) | (sink == order[0]) | (sizes[sink] == 0), 0, jnp.maximum(margin, 0))
    moved = jax.random.randint(jax.random.fold_in(own, 4), (amount // 2,), 0, 1 << 20) % (margin + 1)
    sizes = sizes.at[source_of].add(-moved).at[sink].add(moved)
    items = jnp.searchsorted(jnp.cumsum(sizes), jnp.arange(rows * top), side="right").astype(jnp.int32)
    grid = items.reshape(top, rows).T
    grid = grid[jax.random.permutation(jax.random.fold_in(own, 1), rows)]
    turn = jax.random.randint(jax.random.fold_in(own, 2), (rows, 1), 0, top)
    return jnp.take_along_axis(grid, (jnp.arange(top)[None, :] + turn) % top, axis=1)


def load_shares(count, total, reach, lean, full):
    portions = [(1 << 20) // math.isqrt(rank ** lean) + 1 for rank in range(1, count + 1)]
    largest = reach if full else min(reach, max(-(-total // count), total * portions[0] // sum(portions)))
    least = 1 if total - largest >= count - 1 else 0
    holding, rest = [largest] + [least] * (count - 1), total - largest - least * (count - 1)
    while rest > 0:
        free = [i for i in range(1, count) if holding[i] < largest] or [i for i in range(1, count) if holding[i] < reach]
        whole, budget = sum([portions[i] for i in free]), rest
        for i in free:
            more = min(reach - holding[i], max(1, budget * portions[i] // whole), rest)
            holding[i] = holding[i] + more
            rest = rest - more
    return np.array(holding)


def scatter_about(rng, extent, spread, reach, pieces=(), kind=jnp.bfloat16):
    values = jax.random.normal(rng, extent, jnp.float32) * spread
    if len(pieces) > 0:
        values = shard_levels(rng, extent, pieces, -0.22, 0.18) * values
    return jnp.clip(values, min=-reach, max=reach).astype(kind)


def setup_inputs(seed: int = 0) -> dict:
    arg_keys = jax.random.split(jax.random.key(seed), 13)
    query = draw_query(jax.random.fold_in(arg_keys[12], 71), 0)
    keys_values = draw_keys_values(jax.random.fold_in(arg_keys[12], 71), 0)
    cache = scatter_about(arg_keys[2], (2, CACHED_TOKENS, KEY_VALUE_HEADS * HEAD_SIZE), 1.0, 8.0, ((1, 8), (2, 4)))
    residual = scatter_about(arg_keys[3], (NEW_TOKENS, D), 1.0, 6.0, ((0, 32),))
    out_proj = scatter_about(arg_keys[4], (QUERY_HEADS * HEAD_SIZE, D), (QUERY_HEADS * HEAD_SIZE) ** -0.5, 0.09375, ((0, 4),))
    norm_gain = jnp.clip(1.0 + 0.18 * jax.random.normal(arg_keys[5], (D,), jnp.float32), 0.1, 1.9)
    router = scatter_about(arg_keys[6], (D, EXPERTS), D ** -0.5, 0.09375)
    expert_ids_keys = jax.random.split(jax.random.fold_in(arg_keys[7], 1), NEW_TOKENS // ROWS_DEV)
    expert_ids_turns = jax.random.permutation(jax.random.fold_in(arg_keys[7], 3), NEW_TOKENS // ROWS_DEV)
    expert_ids = jax.vmap(lambda own, number: routed_block(jax.random.fold_in(arg_keys[7], 2), own, number, ROWS_DEV, EXPERTS, 2, CAP, 2))(expert_ids_keys, expert_ids_turns).reshape((NEW_TOKENS, 2))
    w_gate = scatter_about(arg_keys[8], (EXPERTS, D, FF), D ** -0.5, 0.09375, ((0, 4), (2, 8)))
    w_up = scatter_about(arg_keys[9], (EXPERTS, D, FF), D ** -0.5, 0.09375, ((0, 4), (2, 8)))
    w_down = scatter_about(arg_keys[10], (EXPERTS, FF, D), FF ** -0.5, 0.0625, ((0, 4), (1, 8)))
    cotangent = scatter_about(arg_keys[11], (NEW_TOKENS, D), 1.0, 6.0, ((0, 32),))
    return {"query": query, "keys_values": keys_values, "cache": cache, "residual": residual, "out_proj": out_proj, "norm_gain": norm_gain, "router": router, "expert_ids": expert_ids, "w_gate": w_gate, "w_up": w_up, "w_down": w_down, "cotangent": cotangent}


def reference(query, keys_values, cache, residual, out_proj, norm_gain, router, expert_ids, w_gate, w_up, w_down, cotangent):
    head_groups = QUERY_HEADS // KEY_VALUE_HEADS
    query_pos = CACHED_TOKENS + jnp.arange(NEW_TOKENS, dtype=jnp.int32)
    key_pos = jnp.arange(CACHED_TOKENS + NEW_TOKENS, dtype=jnp.int32)
    visible = (key_pos[None, :] <= query_pos[:, None]) & (key_pos[None, :] > query_pos[:, None] - WINDOW)
    key_all = jnp.concatenate([cache[0], keys_values[0]], axis=0)
    value_all = jnp.concatenate([cache[1], keys_values[1]], axis=0)
    score_scale = 1.0 / math.sqrt(HEAD_SIZE)

    def single_head(head_index):
        head_index = head_index.astype(jnp.int32)
        queries = lax.dynamic_slice_in_dim(query, head_index * head_groups * HEAD_SIZE, head_groups * HEAD_SIZE, 1).astype(jnp.float32).reshape(NEW_TOKENS, head_groups, HEAD_SIZE)
        key_rows = lax.dynamic_slice_in_dim(key_all, head_index * HEAD_SIZE, HEAD_SIZE, 1).astype(jnp.float32)
        value_rows = lax.dynamic_slice_in_dim(value_all, head_index * HEAD_SIZE, HEAD_SIZE, 1).astype(jnp.float32)
        scores = jnp.einsum('tjd,kd->tjk', queries, key_rows) * score_scale
        scores = jnp.where(visible[:, None, :], scores, -1e+30)
        row_max = lax.optimization_barrier(jnp.max(scores, axis=-1))
        weights = jnp.where(visible[:, None, :], jnp.exp(scores - row_max[..., None]), 0.0)
        total = lax.optimization_barrier(jnp.sum(weights, axis=-1))
        rounded = lax.optimization_barrier(weights.astype(jnp.bfloat16)).astype(jnp.float32)
        mixed = jnp.einsum('tjk,kd->tjd', rounded, value_rows) / total[..., None]
        return mixed.reshape(NEW_TOKENS, head_groups * HEAD_SIZE)
    per_head_outputs = lax.map(single_head, jnp.arange(KEY_VALUE_HEADS, dtype=jnp.int32))
    attn = jnp.transpose(per_head_outputs, (1, 0, 2)).reshape(NEW_TOKENS, QUERY_HEADS * HEAD_SIZE).astype(jnp.bfloat16)
    hidden_one = residual.astype(jnp.float32) + jnp.dot(attn, out_proj, preferred_element_type=jnp.float32)
    mean_square = lax.optimization_barrier(jnp.mean(hidden_one * hidden_one, axis=-1, keepdims=True))
    normed = (hidden_one * lax.rsqrt(mean_square + 1e-05) * norm_gain).astype(jnp.bfloat16)
    logits = jnp.dot(normed, router, preferred_element_type=jnp.float32)
    onehot = (expert_ids[:, :, None] == jnp.arange(EXPERTS, dtype=jnp.int32)[None, None, :]).astype(jnp.float32)
    chosen = lax.optimization_barrier(jnp.sum(onehot * logits[:, None, :], axis=-1))
    first = 1.0 / (1.0 + jnp.exp(chosen[:, 1] - chosen[:, 0]))
    gates = jnp.stack([first, 1.0 - first], axis=1)
    weight_te = lax.optimization_barrier(jnp.sum(gates[:, :, None] * onehot, axis=1))
    member = lax.optimization_barrier(jnp.sum(onehot, axis=1))
    most_rows = N_CTX * N_EXP * CAP
    group_width = FF // N_CTX
    token_index = jnp.arange(NEW_TOKENS, dtype=jnp.int32)

    def one_expert(combined, inputs):
        gate_mat, up_mat, down_mat, expert_index = inputs
        member_col = jnp.take(member, expert_index, axis=1)
        weight_col = jnp.take(weight_te, expert_index, axis=1)
        keyed = jnp.where(member_col > 0, token_index, NEW_TOKENS + token_index)
        order = jnp.argsort(keyed)[:most_rows].astype(jnp.int32)
        valid = member_col[order]
        rows = jnp.where(valid[:, None] > 0, normed[order], jnp.zeros((), jnp.bfloat16))
        gate_val = jnp.dot(rows, gate_mat, preferred_element_type=jnp.float32)
        up_val = jnp.dot(rows, up_mat, preferred_element_type=jnp.float32)
        hidden_e = (jax.nn.silu(gate_val) * up_val).astype(jnp.bfloat16)
        split_hidden = hidden_e.astype(jnp.float32).reshape(most_rows, N_CTX, group_width)
        split_down = down_mat.astype(jnp.float32).reshape(N_CTX, group_width, D)
        parts = jnp.einsum('rcf,cfd->rcd', split_hidden, split_down)
        parts = lax.optimization_barrier(parts.astype(jnp.bfloat16)).astype(jnp.float32)
        expert_out = lax.optimization_barrier(jnp.sum(parts, axis=1)).astype(jnp.bfloat16).astype(jnp.float32)
        row_weight = weight_col[order] * valid
        combined = combined.at[order].add(row_weight[:, None] * expert_out)
        scaled = (row_weight[:, None] * cotangent[order].astype(jnp.float32)).astype(jnp.bfloat16)
        grad_e = jnp.dot(hidden_e.T, scaled, preferred_element_type=jnp.float32)
        return (combined, grad_e)
    start_sum = jnp.zeros((NEW_TOKENS, D), jnp.float32)
    combined, grad_down = lax.scan(one_expert, start_sum, (w_gate, w_up, w_down, jnp.arange(EXPERTS, dtype=jnp.int32)))
    layer_out = (hidden_one + combined).astype(jnp.bfloat16)
    return (layer_out, grad_down)
```

```python
import functools
import math

import jax
import jax.numpy as jnp
from jax import lax
from jax.experimental import pallas as pl
from jax.experimental.pallas import tpu as pltpu
from jax.sharding import PartitionSpec as P

QUERY_HEADS = 32
KEY_VALUE_HEADS = 8
HEAD_SIZE = 128
WINDOW = 4096
HIDDEN = -1e30
EPSILON = 1e-05


def swap(value, bit):
    return lax.ppermute(value, "ctx", [(i, i ^ bit) for i in range(lax.axis_size("ctx"))])


def from_plane(value, ahead):
    planes = lax.axis_size("exp")
    return lax.ppermute(value, "exp", [(i, (i - ahead) % planes) for i in range(planes)])


def link_bits():
    devices = lax.axis_size("ctx")
    return [1 << b for b in range(1, devices.bit_length() - 1)]


def gather_links(block):
    bits = link_bits()
    if len(bits) != 2:
        held = block
        for bit in bits:
            held = jnp.concatenate([held, swap(held, bit)], axis=0)
        return held
    near, far = bits
    half = block.shape[0] // 2
    first = swap(block, near)
    second = swap(block, far)
    upper = swap(first[:half], far)
    lower = swap(second[half:], near)
    return jnp.concatenate([block, first, second, upper, lower], axis=0)


def plus(a, b):
    return (a.astype(jnp.float32) + b.astype(jnp.float32)).astype(jnp.bfloat16)


def scatter_links(held):
    bits = link_bits()
    rows = held.shape[0] >> len(bits)
    if len(bits) != 2:
        for bit in reversed(bits):
            middle = held.shape[0] // 2
            held = plus(held[:middle], swap(held[middle:], bit))
        return held.astype(jnp.float32)
    near, far = bits
    half = rows // 2
    own, first, second, across = (held[i * rows : (i + 1) * rows] for i in range(4))
    upper = swap(across[:half], far)
    lower = swap(across[half:], near)
    first = jnp.concatenate([plus(first[:half], upper), first[half:]], axis=0)
    second = jnp.concatenate([second[:half], plus(second[half:], lower)], axis=0)
    got_first = swap(first, near)
    got_second = swap(second, far)
    return (
        own.astype(jnp.float32)
        + got_first.astype(jnp.float32)
        + got_second.astype(jnp.float32)
    )


def attend_kernel(slots, cached, window_free, start, final, *refs):
    place = refs[0]
    q_ref = refs[1]
    keys = refs[2 : 2 + slots]
    values = refs[2 + slots : 2 + 2 * slots]
    at = 2 + 2 * slots
    if not start:
        max_in, sum_in, acc_in = refs[at : at + 3]
        at += 3
    if final:
        out_ref = refs[at]
        at += 1
    else:
        max_out, sum_out, acc_out = refs[at : at + 3]
        at += 3
    scores_ref = refs[at]
    tokens = q_ref.shape[0]
    heads = q_ref.shape[1] // HEAD_SIZE
    count = keys[0].shape[1]
    lanes = 128
    power = math.log2(math.e) / math.sqrt(HEAD_SIZE)
    queries = jnp.concatenate(
        [q_ref[:, j * HEAD_SIZE : (j + 1) * HEAD_SIZE] for j in range(heads)], axis=0
    )
    rows = heads * tokens
    new = count - cached
    gap = lax.broadcasted_iota(jnp.int32, (tokens, new), 1) - lax.broadcasted_iota(
        jnp.int32, (tokens, new), 0
    )
    gap = jnp.concatenate([gap] * heads, axis=0)
    if not window_free:
        gap_cached = lax.broadcasted_iota(jnp.int32, (tokens, cached), 1) - (
            lax.broadcasted_iota(jnp.int32, (tokens, cached), 0)
        )
        gap_cached = jnp.concatenate([gap_cached] * heads, axis=0)
    largest = jnp.full((rows, lanes), HIDDEN, jnp.float32)
    for s in range(slots):
        old = lax.dot_general(
            queries,
            keys[s][0, :cached, :],
            (((1,), (1,)), ((), ())),
            preferred_element_type=jnp.float32,
        )
        if not window_free:
            old = jnp.where(gap_cached > place[slots + s], old, HIDDEN)
        fresh = lax.dot_general(
            queries,
            keys[s][0, cached:, :],
            (((1,), (1,)), ((), ())),
            preferred_element_type=jnp.float32,
        )
        seen = gap <= place[s]
        if not window_free:
            seen = seen & (gap > place[s] - WINDOW)
        fresh = jnp.where(seen, fresh, HIDDEN)
        base = s * count
        scores_ref[:, base : base + cached] = old
        scores_ref[:, base + cached : base + count] = fresh
        for j in range(cached // lanes):
            largest = jnp.maximum(largest, old[:, j * lanes : (j + 1) * lanes])
        for j in range(new // lanes):
            largest = jnp.maximum(largest, fresh[:, j * lanes : (j + 1) * lanes])
    top = jnp.max(largest, axis=1, keepdims=True)
    if not start:
        before = max_in[0][:, :1]
        top = jnp.maximum(top, before)
        rescale = jnp.exp2((before - top) * power)
        total = sum_in[0] * rescale
        acc = acc_in[0] * rescale
    else:
        total = jnp.zeros((rows, lanes), jnp.float32)
        acc = jnp.zeros((rows, HEAD_SIZE), jnp.float32)
    for s in range(slots):
        weights = jnp.exp2((scores_ref[:, s * count : (s + 1) * count] - top) * power)
        for j in range(count // lanes):
            total = total + weights[:, j * lanes : (j + 1) * lanes]
        acc = acc + jnp.dot(
            weights.astype(jnp.bfloat16), values[s][0], preferred_element_type=jnp.float32
        )
    if final:
        result = acc / jnp.sum(total, axis=1, keepdims=True)
        for j in range(heads):
            out_ref[:, j * HEAD_SIZE : (j + 1) * HEAD_SIZE] = result[
                j * tokens : (j + 1) * tokens
            ].astype(jnp.bfloat16)
    else:
        max_out[0] = jnp.broadcast_to(top, (rows, lanes))
        sum_out[0] = total
        acc_out[0] = acc


def attend(queries, blocks, places, cached, window_free, state, final):
    slots = len(blocks)
    tokens = queries.shape[0]
    key_arrays = [b[0] for b in blocks]
    value_arrays = [b[1] for b in blocks]
    heads_kv = key_arrays[0][0].shape[2] // HEAD_SIZE
    group = queries.shape[1] // heads_kv
    count = key_arrays[0][0].shape[1]
    rows = tokens * group // HEAD_SIZE

    def plane_spec(plane):
        return pl.BlockSpec((1, count, HEAD_SIZE), lambda h, place, plane=plane: (plane, 0, h))

    carried = pl.BlockSpec((1, rows, HEAD_SIZE), lambda h, place: (h, 0, 0))
    wide = pl.BlockSpec((tokens, group), lambda h, place: (0, h))
    in_specs = [wide]
    in_specs += [plane_spec(p) for _, p in key_arrays]
    in_specs += [plane_spec(p) for _, p in value_arrays]
    operands = [queries] + [a for a, _ in key_arrays] + [a for a, _ in value_arrays]
    if state is not None:
        in_specs += [carried] * 3
        operands += list(state)
    shape = jax.ShapeDtypeStruct((heads_kv, rows, HEAD_SIZE), jnp.float32)
    if final:
        out_specs, out_shape = wide, jax.ShapeDtypeStruct(queries.shape, jnp.bfloat16)
    else:
        out_specs, out_shape = (carried,) * 3, (shape,) * 3
    return pl.pallas_call(
        functools.partial(attend_kernel, slots, cached, window_free, state is None, final),
        out_shape=out_shape,
        grid_spec=pltpu.PrefetchScalarGridSpec(
            num_scalar_prefetch=1,
            grid=(heads_kv,),
            in_specs=in_specs,
            out_specs=out_specs,
            scratch_shapes=[pltpu.VMEM((rows, slots * count), jnp.float32)],
        ),
        name="attend",
    )(places, *operands)


def attention(query, keys_values, cache):
    ctx_size = lax.axis_size("ctx")
    here = lax.axis_index("ctx")
    tokens = query.shape[0]
    cached = cache.shape[1]
    window_free = (cached + tokens) * ctx_size <= WINDOW

    def places(offsets):
        new, old = [], []
        for s in offsets:
            owner = here ^ s
            new.append((here - owner) * tokens)
            old.append(cached * ctx_size + here * tokens - owner * cached - WINDOW)
        return jnp.stack(new + old).astype(jnp.int32)

    stage = functools.partial(attend, query, cached=cached, window_free=window_free)
    own = jnp.concatenate([cache, keys_values], axis=1)
    bits = link_bits()
    whole = lambda a: ((a, 0), (a, 1))
    if len(bits) != 2:
        held = [own]
        for bit in [1] + bits:
            held = held + [swap(a, bit) for a in held]
        state = None
        for s, a in enumerate(held):
            state = stage([whole(a)], places([s]), state=state, final=s == len(held) - 1)
        return state
    near, far = bits
    first = swap(own, near)
    second = swap(own, far)
    mate = swap(own, 1)
    across_k = swap(first[:1], far)
    across_v = swap(second[1:], near)
    mate_first = swap(first, 1)
    mate_second = swap(second, 1)
    mate_k = swap(across_k, 1)
    mate_v = swap(across_v, 1)
    state = stage([whole(own), whole(mate)], places([0, 1]), state=None, final=False)
    state = stage(
        [whole(first), whole(second), whole(mate_first), whole(mate_second)],
        places([near, far, near ^ 1, far ^ 1]),
        state=state,
        final=False,
    )
    return stage(
        [((across_k, 0), (across_v, 0)), ((mate_k, 0), (mate_v, 0))],
        places([near ^ far, near ^ far ^ 1]),
        state=state,
        final=True,
    )


def on_device(
    query,
    keys_values,
    cache,
    residual,
    out_proj,
    norm_gain,
    router,
    expert_ids,
    w_gate,
    w_up,
    w_down,
    cotangent,
):
    ctx_size = lax.axis_size("ctx")
    planes = lax.axis_size("exp")
    plane = lax.axis_index("exp")
    experts = router.shape[1]
    row_count, width = residual.shape

    stacked = jnp.concatenate(
        [cotangent] + [from_plane(cotangent, k) for k in range(1, planes)], axis=0
    )
    grad_links = gather_links(stacked)
    grad_mate = swap(grad_links, 1)

    attn = attention(query, keys_values, cache)

    partial = jnp.dot(attn, out_proj, preferred_element_type=jnp.float32)
    partial = partial.reshape(planes, row_count, width)
    hidden_one = residual.astype(jnp.float32) + lax.dynamic_index_in_dim(
        partial, plane, 0, keepdims=False
    )
    for k in range(1, planes):
        rows = lax.dynamic_index_in_dim(partial, (plane - k) % planes, 0, keepdims=False)
        hidden_one = hidden_one + from_plane(rows.astype(jnp.bfloat16), k).astype(jnp.float32)
    mean_square = jnp.mean(hidden_one * hidden_one, axis=-1, keepdims=True)
    normed = (hidden_one * lax.rsqrt(mean_square + EPSILON) * norm_gain).astype(jnp.bfloat16)

    logits = jnp.dot(normed, router, preferred_element_type=jnp.float32)
    onehot = (expert_ids[:, :, None] == jnp.arange(experts, dtype=jnp.int32)).astype(jnp.float32)
    chosen = jnp.sum(onehot * logits[:, None, :], axis=-1)
    gate_first = 1.0 / (1.0 + jnp.exp(chosen[:, 1] - chosen[:, 0]))
    gates = jnp.stack([gate_first, 1.0 - gate_first], axis=1)
    gate_of = jnp.sum(gates[:, :, None] * onehot, axis=1)

    def gate_for(ahead):
        return lax.dynamic_index_in_dim(gate_of, (plane + ahead) % planes, 1, keepdims=False)

    weights = jnp.stack(
        [gate_for(0)] + [from_plane(gate_for(-k), k) for k in range(1, planes)], axis=0
    )
    weights = weights.reshape(1, planes, row_count)
    for bit in link_bits() + [1]:
        weights = jnp.concatenate([weights, swap(weights, bit)], axis=0)

    gate_mat = w_gate[0]
    up_mat = w_up[0]
    down_mat = w_down[0]
    blocks = [normed] + [from_plane(normed, k) for k in range(1, planes)]
    hidden = []
    combined = jnp.zeros((row_count, width), jnp.float32)
    for k in range(planes):
        links = gather_links(blocks[k])
        rows = jnp.concatenate([links, swap(links, 1)], axis=0)
        gate_val = jnp.dot(rows, gate_mat, preferred_element_type=jnp.float32)
        up_val = jnp.dot(rows, up_mat, preferred_element_type=jnp.float32)
        hidden_k = (jax.nn.silu(gate_val) * up_val).astype(jnp.bfloat16)
        hidden.append(hidden_k)
        part = jnp.dot(hidden_k, down_mat, preferred_element_type=jnp.float32)
        part = part.astype(jnp.bfloat16)
        middle = part.shape[0] // 2
        summed = scatter_links(plus(part[:middle], swap(part[middle:], 1)))
        summed = summed.astype(jnp.bfloat16)
        if k:
            summed = from_plane(summed, -k)
        combined = combined + gate_for(-k)[:, None] * summed.astype(jnp.float32)
    layer_out = (hidden_one + combined).astype(jnp.bfloat16)

    grads = jnp.concatenate([grad_links, grad_mate], axis=0)
    scaled = (weights.reshape(-1)[:, None] * grads.astype(jnp.float32)).astype(jnp.bfloat16)
    units = gate_mat.shape[1]
    hidden_all = jnp.stack(hidden, axis=0).reshape(planes, ctx_size, row_count, units)
    hidden_all = jnp.swapaxes(hidden_all, 0, 1).reshape(planes * ctx_size * row_count, units)
    gradient = lax.dot_general(
        hidden_all, scaled, (((0,), (0,)), ((), ())), preferred_element_type=jnp.float32
    )
    return (layer_out, gradient[None])


def solution(mesh):
    placed = (
        P("ctx", "exp"),
        P(None, "ctx", "exp"),
        P(None, "ctx", "exp"),
        P(("ctx", "exp"), None),
        P("exp", None),
        P(),
        P(),
        P(("ctx", "exp"), None),
        P("exp", None, "ctx"),
        P("exp", None, "ctx"),
        P("exp", "ctx", None),
        P(("ctx", "exp"), None),
    )
    return jax.shard_map(
        on_device,
        mesh=mesh,
        in_specs=placed,
        out_specs=(P(("ctx", "exp"), None), P("exp", "ctx", None)),
        check_vma=False,
    )
```

```python
import functools
import math

import jax
import jax.numpy as jnp
from jax import lax
from jax.experimental import pallas as pl
from jax.experimental.pallas import tpu as pltpu
from jax.sharding import PartitionSpec as P


HEAD_SIZE = 128
WINDOW = 4096
HIDDEN = -1e30
EPSILON = 1e-05


def swap(value, bit):
    return lax.ppermute(value, "ctx", [(i, i ^ bit) for i in range(lax.axis_size("ctx"))])


def swap_plane(value, bits):
    return lax.ppermute(value, "exp", [(i, i ^ bits) for i in range(lax.axis_size("exp"))])


def link_bits():
    devices = lax.axis_size("ctx")
    return [1 << b for b in range(1, devices.bit_length() - 1)]


def cross(value, turn):
    near, far = link_bits()
    even, odd = (near, far) if turn == 0 else (far, near)
    pairs = [(i, i ^ (odd if i % 2 else even)) for i in range(lax.axis_size("ctx"))]
    return lax.ppermute(value, "ctx", pairs)


def gather(block):
    bits = link_bits()
    if len(bits) != 2:
        held = block
        for bit in bits + [1]:
            held = jnp.concatenate([held, swap(held, bit)], axis=0)
        return [held]
    rows = block.shape[0]
    pair = jnp.concatenate([block, swap(block, 1)], axis=0)
    beside = cross(pair, 0)
    opposite = cross(beside[:rows], 1)
    sent = jnp.concatenate([beside, opposite], axis=0)
    return [pair, sent, swap(sent, 1)]


def plus(a, b):
    return (a.astype(jnp.float32) + b.astype(jnp.float32)).astype(jnp.bfloat16)


def scatter(parts):
    bits = link_bits()
    if len(bits) != 2:
        held = parts[0]
        for bit in [1] + bits[::-1]:
            middle = held.shape[0] // 2
            held = plus(held[:middle], swap(held[middle:], bit))
        return held
    pair, sent, theirs = parts
    rows = pair.shape[0] // 2
    got = swap(theirs, 1)
    returned = cross(plus(sent[2 * rows :], got[2 * rows :]), 1)
    beside = plus(sent[: 2 * rows], got[: 2 * rows])
    beside = jnp.concatenate([plus(beside[:rows], returned), beside[rows:]], axis=0)
    pair = plus(pair, cross(beside, 0))
    return plus(pair[:rows], swap(pair[rows:], 1))


def expert_kernel(parts, steps, place, tags_ref, router_ref, *refs):
    rows_refs = refs[:parts]
    gate_ref, up_ref, down_ref = refs[parts : parts + 3]
    part_refs = refs[parts + 3 : 2 * parts + 3]
    turned_ref, rows_all, weight_ref, hidden_ref = refs[2 * parts + 3 :]
    step = pl.program_id(0)
    wide = gate_ref.shape[1]

    @pl.when(step == 0)
    def _():
        at = 0
        for ref in rows_refs:
            rows_all[at : at + ref.shape[0]] = ref[...]
            at += ref.shape[0]
        logits = jnp.dot(rows_all[...], router_ref[...], preferred_element_type=jnp.float32)
        lane = lax.broadcasted_iota(jnp.int32, logits.shape, 1).astype(jnp.float32)
        tags = tags_ref[...].astype(jnp.float32)
        one, two = tags[:, :1], tags[:, 1:2]
        first = jnp.sum(jnp.where(lane == one, logits, 0.0), axis=1, keepdims=True)
        second = jnp.sum(jnp.where(lane == two, logits, 0.0), axis=1, keepdims=True)
        gate = 1.0 / (1.0 + jnp.exp(second - first))
        mine = place[0].astype(jnp.float32)
        weight = jnp.where(one == mine, gate, 0.0) + jnp.where(two == mine, 1.0 - gate, 0.0)
        weight_ref[...] = jnp.broadcast_to(weight, weight_ref.shape)

    @pl.when(step < steps)
    def _():
        rows = rows_all[...]
        gate = jnp.dot(rows, gate_ref[...], preferred_element_type=jnp.float32)
        up = jnp.dot(rows, up_ref[...], preferred_element_type=jnp.float32)
        hidden = gate / (1.0 + jnp.exp(-gate)) * up * weight_ref[:, :1]
        hidden = hidden.astype(jnp.bfloat16)
        hidden_ref[:, pl.ds(pl.multiple_of(step * wide, wide), wide)] = hidden
        turned_ref[...] = hidden.T

    @pl.when(step >= steps)
    def _():
        part = jnp.dot(hidden_ref[...], down_ref[...], preferred_element_type=jnp.float32)
        part = part.astype(jnp.bfloat16)
        at = 0
        for ref in part_refs:
            ref[...] = part[at : at + ref.shape[0]]
            at += ref.shape[0]


def expert(place, tags, router, rows, gate_mat, up_mat, down_mat):
    width, units = gate_mat.shape
    experts = router.shape[1]
    router = jnp.pad(router, ((0, 0), (0, HEAD_SIZE - experts)))
    count = sum(r.shape[0] for r in rows)
    wide, broad = min(256, units), min(1024, width)
    steps, turns = units // wide, width // broad
    whole = lambda shape: pl.BlockSpec(
        shape, lambda i, place: (0, 0), pipeline_mode=pl.Buffered(1)
    )
    late = lambda i, place: (0, jnp.maximum(i - steps, 0))
    early = lambda i, place: (0, jnp.minimum(i, steps - 1))
    return pl.pallas_call(
        functools.partial(expert_kernel, len(rows), steps),
        out_shape=[jax.ShapeDtypeStruct(r.shape, jnp.bfloat16) for r in rows]
        + [jax.ShapeDtypeStruct((units, count), jnp.bfloat16)],
        grid_spec=pltpu.PrefetchScalarGridSpec(
            num_scalar_prefetch=1,
            grid=(steps + turns,),
            in_specs=[whole(tags.shape), whole(router.shape)]
            + [whole(r.shape) for r in rows]
            + [pl.BlockSpec((width, wide), early)] * 2
            + [pl.BlockSpec((units, broad), late)],
            out_specs=[pl.BlockSpec((r.shape[0], broad), late) for r in rows]
            + [pl.BlockSpec((wide, count), lambda i, place: (jnp.minimum(i, steps - 1), 0))],
            scratch_shapes=[
                pltpu.VMEM((count, width), jnp.bfloat16),
                pltpu.VMEM((count, HEAD_SIZE), jnp.float32),
                pltpu.VMEM((count, units), jnp.bfloat16),
            ],
        ),
        compiler_params=pltpu.CompilerParams(vmem_limit_bytes=36 << 20),
        cost_estimate=pl.CostEstimate(
            flops=6 * count * width * units,
            transcendentals=count * units,
            bytes_accessed=2 * (3 * width * units + 2 * count * width),
        ),
        name="expert",
    )(place, tags, router, *rows, gate_mat, up_mat, down_mat)


def outer_kernel(parts, pieces, blocks, *refs):
    grad_refs = refs[:parts]
    turned_refs = refs[parts : parts + pieces]
    out_ref, grads_ref = refs[parts + pieces :]
    length = grads_ref.shape[1] // blocks
    block = 0
    for ref in grad_refs:
        for at in range(0, ref.shape[0], pieces * length):
            for piece in range(pieces):
                start = at + piece * length
                grads_ref[piece, block * length : (block + 1) * length] = ref[
                    start : start + length
                ]
            block += 1
    total = jnp.dot(turned_refs[0][...], grads_ref[0], preferred_element_type=jnp.float32)
    for piece in range(1, pieces):
        total += jnp.dot(
            turned_refs[piece][...], grads_ref[piece], preferred_element_type=jnp.float32
        )
    out_ref[...] = total


def outer(grads, turned, blocks, width):
    units, count = turned[0].shape
    broad = min(512, width)
    pieces = len(turned)
    return pl.pallas_call(
        functools.partial(outer_kernel, len(grads), pieces, blocks),
        out_shape=jax.ShapeDtypeStruct((units, width), jnp.float32),
        grid=(width // broad,),
        in_specs=[pl.BlockSpec((g.shape[0], broad), lambda i: (0, i)) for g in grads]
        + [
            pl.BlockSpec((units, count), lambda i: (0, 0), pipeline_mode=pl.Buffered(1))
            for _ in turned
        ],
        out_specs=pl.BlockSpec((units, broad), lambda i: (0, i)),
        scratch_shapes=[pltpu.VMEM((pieces, count, broad), jnp.bfloat16)],
        compiler_params=pltpu.CompilerParams(vmem_limit_bytes=24 << 20),
        cost_estimate=pl.CostEstimate(
            flops=2 * units * count * pieces * width,
            transcendentals=0,
            bytes_accessed=4 * units * width + 4 * count * pieces * width,
        ),
        name="outer",
    )(*grads, *turned)


def attend_kernel(slots, cached, window_free, start, final, *refs):
    place = refs[0]
    q_ref = refs[1]
    keys = refs[2 : 2 + slots]
    values = refs[2 + slots : 2 + 2 * slots]
    at = 2 + 2 * slots
    if not start:
        max_in, sum_in, acc_in = refs[at : at + 3]
        at += 3
    if final:
        out_ref = refs[at]
        at += 1
    else:
        max_out, sum_out, acc_out = refs[at : at + 3]
        at += 3
    scores_ref = refs[at]
    tokens = q_ref.shape[0]
    heads = q_ref.shape[1] // HEAD_SIZE
    count = keys[0].shape[1]
    lanes = 128
    power = math.log2(math.e) / math.sqrt(HEAD_SIZE)
    queries = jnp.concatenate(
        [q_ref[:, j * HEAD_SIZE : (j + 1) * HEAD_SIZE] for j in range(heads)], axis=0
    )
    rows = heads * tokens
    new = count - cached
    gap = lax.broadcasted_iota(jnp.int32, (tokens, new), 1) - lax.broadcasted_iota(
        jnp.int32, (tokens, new), 0
    )
    gap = jnp.concatenate([gap] * heads, axis=0)
    if not window_free:
        gap_cached = lax.broadcasted_iota(jnp.int32, (tokens, cached), 1) - (
            lax.broadcasted_iota(jnp.int32, (tokens, cached), 0)
        )
        gap_cached = jnp.concatenate([gap_cached] * heads, axis=0)
    largest = jnp.full((rows, lanes), HIDDEN, jnp.float32)
    for s in range(slots):
        old = lax.dot_general(
            queries,
            keys[s][0, :cached, :],
            (((1,), (1,)), ((), ())),
            preferred_element_type=jnp.float32,
        )
        if not window_free:
            old = jnp.where(gap_cached > place[slots + s], old, HIDDEN)
        fresh = lax.dot_general(
            queries,
            keys[s][0, cached:, :],
            (((1,), (1,)), ((), ())),
            preferred_element_type=jnp.float32,
        )
        seen = gap <= place[s]
        if not window_free:
            seen = seen & (gap > place[s] - WINDOW)
        fresh = jnp.where(seen, fresh, HIDDEN)
        base = s * count
        scores_ref[:, base : base + cached] = old
        scores_ref[:, base + cached : base + count] = fresh
        for j in range(cached // lanes):
            largest = jnp.maximum(largest, old[:, j * lanes : (j + 1) * lanes])
        for j in range(new // lanes):
            largest = jnp.maximum(largest, fresh[:, j * lanes : (j + 1) * lanes])
    top = jnp.max(largest, axis=1, keepdims=True)
    if not start:
        before = max_in[0][:, :1]
        top = jnp.maximum(top, before)
        rescale = jnp.exp2((before - top) * power)
        total = sum_in[0] * rescale
        acc = acc_in[0] * rescale
    else:
        total = jnp.zeros((rows, lanes), jnp.float32)
        acc = jnp.zeros((rows, HEAD_SIZE), jnp.float32)
    for s in range(slots):
        weights = jnp.exp2((scores_ref[:, s * count : (s + 1) * count] - top) * power)
        for j in range(count // lanes):
            total = total + weights[:, j * lanes : (j + 1) * lanes]
        acc = acc + jnp.dot(
            weights.astype(jnp.bfloat16), values[s][0], preferred_element_type=jnp.float32
        )
    if final:
        result = acc / jnp.sum(total, axis=1, keepdims=True)
        for j in range(heads):
            out_ref[:, j * HEAD_SIZE : (j + 1) * HEAD_SIZE] = result[
                j * tokens : (j + 1) * tokens
            ].astype(jnp.bfloat16)
    else:
        max_out[0] = jnp.broadcast_to(top, (rows, lanes))
        sum_out[0] = total
        acc_out[0] = acc


def attend(queries, blocks, places, cached, window_free, state, final):
    slots = len(blocks)
    tokens = queries.shape[0]
    key_arrays = [b[0] for b in blocks]
    value_arrays = [b[1] for b in blocks]
    heads_kv = key_arrays[0][0].shape[2] // HEAD_SIZE
    group = queries.shape[1] // heads_kv
    count = key_arrays[0][0].shape[1]
    rows = tokens * group // HEAD_SIZE

    def plane_spec(plane):
        return pl.BlockSpec((1, count, HEAD_SIZE), lambda h, place, plane=plane: (plane, 0, h))

    carried = pl.BlockSpec((1, rows, HEAD_SIZE), lambda h, place: (h, 0, 0))
    wide = pl.BlockSpec((tokens, group), lambda h, place: (0, h))
    in_specs = [wide]
    in_specs += [plane_spec(p) for _, p in key_arrays]
    in_specs += [plane_spec(p) for _, p in value_arrays]
    operands = [queries] + [a for a, _ in key_arrays] + [a for a, _ in value_arrays]
    if state is not None:
        in_specs += [carried] * 3
        operands += list(state)
    shape = jax.ShapeDtypeStruct((heads_kv, rows, HEAD_SIZE), jnp.float32)
    if final:
        out_specs, out_shape = wide, jax.ShapeDtypeStruct(queries.shape, jnp.bfloat16)
    else:
        out_specs, out_shape = (carried,) * 3, (shape,) * 3
    work = queries.shape[0] * queries.shape[1] * slots * count
    return pl.pallas_call(
        functools.partial(attend_kernel, slots, cached, window_free, state is None, final),
        out_shape=out_shape,
        grid_spec=pltpu.PrefetchScalarGridSpec(
            num_scalar_prefetch=1,
            grid=(heads_kv,),
            in_specs=in_specs,
            out_specs=out_specs,
            scratch_shapes=[pltpu.VMEM((rows, slots * count), jnp.float32)],
        ),
        cost_estimate=pl.CostEstimate(
            flops=4 * work, transcendentals=work // HEAD_SIZE, bytes_accessed=work // 64
        ),
        name="attend",
    )(places, *operands)


def attention(query, keys_values, cache):
    ctx_size = lax.axis_size("ctx")
    here = lax.axis_index("ctx")
    tokens = query.shape[0]
    cached = cache.shape[1]
    window_free = (cached + tokens) * ctx_size <= WINDOW

    def places(offsets):
        new, old = [], []
        for s in offsets:
            owner = here ^ s
            new.append((here - owner) * tokens)
            old.append(cached * ctx_size + here * tokens - owner * cached - WINDOW)
        return jnp.stack(new + old).astype(jnp.int32)

    stage = functools.partial(attend, query, cached=cached, window_free=window_free)
    own = jnp.concatenate([cache, keys_values], axis=1)
    bits = link_bits()
    if len(bits) != 2:
        held = [(own, 0)]
        for bit in [1] + bits:
            held = held + [(swap(a, bit), s ^ bit) for a, s in held]
        state = None
        for index, (a, s) in enumerate(held):
            last = index == len(held) - 1
            state = stage([((a, 0), (a, 1))], places([s]), state=state, final=last)
        return state
    parity = here % 2
    near = jnp.where(parity == 0, bits[0], bits[1])
    far = jnp.where(parity == 0, bits[1], bits[0])
    mate = swap(own, 1)
    pair = jnp.concatenate([own, mate], axis=0)
    beside = cross(pair, 0)
    opposite = cross(beside[:2], 1)
    mate_beside = swap(beside, 1)
    mate_opposite = swap(opposite, 1)
    slot = lambda a, i: ((a, 2 * i), (a, 2 * i + 1))
    state = stage([slot(pair, 0), slot(pair, 1)], places([0, 1]), state=None, final=False)
    state = stage(
        [slot(beside, 0), slot(beside, 1), slot(mate_beside, 0), slot(mate_beside, 1)],
        places([near, near ^ 1, far ^ 1, far]),
        state=state,
        final=False,
    )
    return stage(
        [slot(opposite, 0), slot(mate_opposite, 0)],
        places([near ^ far, near ^ far ^ 1]),
        state=state,
        final=True,
    )


def planes_of(value):
    blocks = [value]
    for k in range(1, lax.axis_size("exp")):
        source, bits = (value, k) if k == 1 or k % 2 == 0 else (blocks[k - 1], 1)
        blocks.append(swap_plane(source, bits))
    return blocks


def on_device(
    query,
    keys_values,
    cache,
    residual,
    out_proj,
    norm_gain,
    router,
    expert_ids,
    w_gate,
    w_up,
    w_down,
    cotangent,
):
    ctx_size = lax.axis_size("ctx")
    planes = lax.axis_size("exp")
    plane = lax.axis_index("exp")
    row_count, width = residual.shape

    tags = jnp.pad(expert_ids.astype(jnp.bfloat16), ((0, 0), (0, HEAD_SIZE - 2)))
    tagged = planes_of(jnp.concatenate([cotangent, tags], axis=1))
    grads = gather(jnp.concatenate(tagged, axis=0))
    ids = jnp.concatenate([g[:, width:] for g in grads], axis=0)
    ids = ids.reshape(ctx_size, planes, row_count, HEAD_SIZE)

    attn = attention(query, keys_values, cache)

    partial = jnp.dot(attn, out_proj, preferred_element_type=jnp.float32)
    partial = partial.reshape(planes, row_count, width)

    def share(k):
        return lax.dynamic_index_in_dim(partial, plane ^ k, 0, keepdims=False)

    hidden_one = residual.astype(jnp.float32) + share(0)
    for k in range(0, planes, 2):
        both = swap_plane(share(k + 1).astype(jnp.bfloat16), 1)
        if k:
            both = swap_plane((share(k) + both.astype(jnp.float32)).astype(jnp.bfloat16), k)
        hidden_one = hidden_one + both.astype(jnp.float32)
    mean_square = jnp.mean(hidden_one * hidden_one, axis=-1, keepdims=True)
    normed = (hidden_one * lax.rsqrt(mean_square + EPSILON) * norm_gain).astype(jnp.bfloat16)

    gate_mat = w_gate[0]
    up_mat = w_up[0]
    down_mat = w_down[0]
    place = jnp.full((1,), plane, jnp.int32)
    blocks = planes_of(normed)
    turned = []
    layer = hidden_one
    for k in range(0, planes, 2):
        rows = gather(jnp.concatenate(blocks[k : k + 2], axis=0))
        tags = ids[:, k : k + 2].reshape(-1, HEAD_SIZE)
        *parts, turned_piece = expert(
            place, tags, router, rows, gate_mat, up_mat, down_mat
        )
        turned.append(turned_piece)
        summed = scatter(parts)
        both = plus(summed[:row_count], swap_plane(summed[row_count:], 1))
        if k:
            both = swap_plane(both, k)
        layer = layer + both.astype(jnp.float32)
    layer_out = layer.astype(jnp.bfloat16)

    gradient = outer(grads, turned, ctx_size, width)
    return (layer_out, gradient[None])


def solution(mesh):
    placed = (
        P("ctx", "exp"),
        P(None, "ctx", "exp"),
        P(None, "ctx", "exp"),
        P(("ctx", "exp"), None),
        P("exp", None),
        P(),
        P(),
        P(("ctx", "exp"), None),
        P("exp", None, "ctx"),
        P("exp", None, "ctx"),
        P("exp", "ctx", None),
        P(("ctx", "exp"), None),
    )

    return jax.shard_map(
        on_device,
        mesh=mesh,
        in_specs=placed,
        out_specs=(P(("ctx", "exp"), None), P("exp", "ctx", None)),
        check_vma=False,
    )
```

```python
import functools
import math

import jax
import jax.numpy as jnp
from jax import lax
from jax.experimental import pallas as pl
from jax.experimental.pallas import tpu as pltpu
from jax.sharding import PartitionSpec as P


HEAD_SIZE = 128
WINDOW = 4096
HIDDEN = -1e30
EPSILON = 1e-05


def swap(value, bit):
    return lax.ppermute(value, "ctx", [(i, i ^ bit) for i in range(lax.axis_size("ctx"))])


def swap_plane(value, bits):
    return lax.ppermute(value, "exp", [(i, i ^ bits) for i in range(lax.axis_size("exp"))])


def link_bits():
    devices = lax.axis_size("ctx")
    return [1 << b for b in range(1, devices.bit_length() - 1)]


def cross(value, turn):
    near, far = link_bits()
    even, odd = (near, far) if turn == 0 else (far, near)
    pairs = [(i, i ^ (odd if i % 2 else even)) for i in range(lax.axis_size("ctx"))]
    return lax.ppermute(value, "ctx", pairs)


def gather(block):
    bits = link_bits()
    if len(bits) != 2:
        held = block
        for bit in bits + [1]:
            held = jnp.concatenate([held, swap(held, bit)], axis=0)
        return [held]
    beside = cross(block, 0)
    mate = swap(block, 1)
    beside_mate = cross(mate, 0)
    opposite = cross(beside, 1)
    return [
        block,
        mate,
        beside,
        beside_mate,
        opposite,
        swap(beside, 1),
        swap(beside_mate, 1),
        swap(opposite, 1),
    ]


def plus(a, b):
    return (a.astype(jnp.float32) + b.astype(jnp.float32)).astype(jnp.bfloat16)


def scatter(parts):
    bits = link_bits()
    if len(bits) != 2:
        held = parts[0]
        for bit in [1] + bits[::-1]:
            middle = held.shape[0] // 2
            held = plus(held[:middle], swap(held[middle:], bit))
        return held
    own, mate, beside, beside_mate, opposite, *theirs = parts
    opposite = plus(opposite, swap(theirs[2], 1))
    returned = cross(opposite, 1)
    beside_mate = plus(beside_mate, swap(theirs[1], 1))
    mate = plus(mate, cross(beside_mate, 0))
    beside = plus(plus(beside, swap(theirs[0], 1)), returned)
    own = plus(own, swap(mate, 1))
    return plus(own, cross(beside, 0))


def rise_kernel(parts, planes, place, router_ref, *refs):
    tag_refs, rows_refs = refs[:parts], refs[parts : 2 * parts]
    gate_ref, up_ref, hidden_ref, turned_ref, rows_all, weight_ref, tags_ref = refs[2 * parts :]

    @pl.when(pl.program_id(0) == 0)
    def _():
        at = 0
        for ref in rows_refs:
            rows_all[at : at + ref.shape[0]] = ref[...]
            at += ref.shape[0]
        first_plane, last_plane, length = planes
        at = 0
        for ref in tag_refs:
            for base in range(0, ref.shape[0], length[0]):
                for k in range(first_plane, last_plane):
                    start = base + k * length[1]
                    tags_ref[at : at + length[1]] = ref[start : start + length[1]]
                    at += length[1]
        logits = jnp.dot(rows_all[...], router_ref[...], preferred_element_type=jnp.float32)
        lane = lax.broadcasted_iota(jnp.int32, logits.shape, 1).astype(jnp.float32)
        tags = tags_ref[...].astype(jnp.float32)
        one, two = tags[:, :1], tags[:, 1:2]
        first = jnp.sum(jnp.where(lane == one, logits, 0.0), axis=1, keepdims=True)
        second = jnp.sum(jnp.where(lane == two, logits, 0.0), axis=1, keepdims=True)
        gate = 1.0 / (1.0 + jnp.exp(second - first))
        mine = place[0].astype(jnp.float32)
        weight = jnp.where(one == mine, gate, 0.0) + jnp.where(two == mine, 1.0 - gate, 0.0)
        weight_ref[...] = jnp.broadcast_to(weight, weight_ref.shape)

    rows = rows_all[...]
    gate = jnp.dot(rows, gate_ref[...], preferred_element_type=jnp.float32)
    up = jnp.dot(rows, up_ref[...], preferred_element_type=jnp.float32)
    hidden = gate / (1.0 + jnp.exp(-gate)) * up * weight_ref[:, :1]
    hidden = hidden.astype(jnp.bfloat16)
    hidden_ref[...] = hidden
    turned_ref[...] = hidden.T


def rise(place, grads, planes, router, rows, gate_mat, up_mat):
    width, units = gate_mat.shape
    tag = lambda g: pl.BlockSpec(
        (g.shape[0], HEAD_SIZE),
        lambda i, place: (0, width // HEAD_SIZE),
        pipeline_mode=pl.Buffered(1),
    )
    count = sum(r.shape[0] for r in rows)
    wide = min(256, units)
    whole = lambda shape: pl.BlockSpec(
        shape, lambda i, place: (0, 0), pipeline_mode=pl.Buffered(1)
    )
    column = lambda i, place: (0, i)
    return pl.pallas_call(
        functools.partial(rise_kernel, len(rows), planes),
        out_shape=[
            jax.ShapeDtypeStruct((count, units), jnp.bfloat16),
            jax.ShapeDtypeStruct((units, count), jnp.bfloat16),
        ],
        grid_spec=pltpu.PrefetchScalarGridSpec(
            num_scalar_prefetch=1,
            grid=(units // wide,),
            in_specs=[whole(router.shape)]
            + [tag(g) for g in grads]
            + [whole(r.shape) for r in rows]
            + [pl.BlockSpec((width, wide), column)] * 2,
            out_specs=[
                pl.BlockSpec((count, wide), column),
                pl.BlockSpec((wide, count), lambda i, place: (i, 0)),
            ],
            scratch_shapes=[
                pltpu.VMEM((count, width), jnp.bfloat16),
                pltpu.VMEM((count, HEAD_SIZE), jnp.float32),
                pltpu.VMEM((count, HEAD_SIZE), jnp.bfloat16),
            ],
        ),
        compiler_params=pltpu.CompilerParams(vmem_limit_bytes=28 << 20),
        cost_estimate=pl.CostEstimate(
            flops=4 * count * width * units,
            transcendentals=count * units,
            bytes_accessed=2 * (2 * width * units + count * width),
        ),
        name="rise",
    )(place, router, *grads, *rows, gate_mat, up_mat)


def fall_kernel(hidden_ref, down_ref, *part_refs):
    part = jnp.dot(hidden_ref[...], down_ref[...], preferred_element_type=jnp.float32)
    part = part.astype(jnp.bfloat16)
    at = 0
    for ref in part_refs:
        ref[...] = part[at : at + ref.shape[0]]
        at += ref.shape[0]


def fall(hidden, down_mat, counts):
    units, width = down_mat.shape
    broad = min(1024, width)
    column = lambda i: (0, i)
    return pl.pallas_call(
        fall_kernel,
        out_shape=[jax.ShapeDtypeStruct((c, width), jnp.bfloat16) for c in counts],
        grid=(width // broad,),
        in_specs=[
            pl.BlockSpec(hidden.shape, lambda i: (0, 0), pipeline_mode=pl.Buffered(1)),
            pl.BlockSpec((units, broad), column),
        ],
        out_specs=[pl.BlockSpec((c, broad), column) for c in counts],
        compiler_params=pltpu.CompilerParams(vmem_limit_bytes=20 << 20),
        cost_estimate=pl.CostEstimate(
            flops=2 * sum(counts) * width * units,
            transcendentals=0,
            bytes_accessed=2 * (width * units + sum(counts) * width),
        ),
        name="fall",
    )(hidden, down_mat)


def project_kernel(planes, place, attn_ref, proj_ref, residual_ref, own_ref, *refs):
    share_refs, sums_ref = refs[:-1], refs[-1]
    rows = own_ref.shape[0]
    sums_ref[...] = jnp.dot(attn_ref[...], proj_ref[...], preferred_element_type=jnp.float32)
    for k in range(planes):
        start = pl.multiple_of((place[0] ^ k) * rows, rows)
        share = sums_ref[pl.ds(start, rows), :]
        if k:
            share_refs[k - 1][...] = share.astype(share_refs[k - 1].dtype)
        else:
            own_ref[...] = share + residual_ref[...].astype(jnp.float32)


def project(place, attn, out_proj, residual):
    rows, width = residual.shape
    tokens = attn.shape[0]
    planes = tokens // rows
    broad = min(1024, width)
    column = lambda i, place: (0, i)
    small = pl.BlockSpec((rows, broad), column)
    return pl.pallas_call(
        functools.partial(project_kernel, planes),
        out_shape=[jax.ShapeDtypeStruct((rows, width), jnp.float32)]
        + [
            jax.ShapeDtypeStruct((rows, width), jnp.bfloat16 if k % 2 else jnp.float32)
            for k in range(1, planes)
        ],
        grid_spec=pltpu.PrefetchScalarGridSpec(
            num_scalar_prefetch=1,
            grid=(width // broad,),
            in_specs=[
                pl.BlockSpec(attn.shape, lambda i, place: (0, 0)),
                pl.BlockSpec((out_proj.shape[0], broad), column),
                small,
            ],
            out_specs=[small] * planes,
            scratch_shapes=[pltpu.VMEM((tokens, broad), jnp.float32)],
        ),
        compiler_params=pltpu.CompilerParams(vmem_limit_bytes=16 << 20),
        cost_estimate=pl.CostEstimate(
            flops=2 * tokens * out_proj.shape[0] * width,
            transcendentals=0,
            bytes_accessed=2 * out_proj.shape[0] * width,
        ),
        name="project",
    )(place, attn, out_proj, residual)


def outer_kernel(parts, pieces, blocks, *refs):
    grad_refs = refs[:parts]
    turned_refs = refs[parts : parts + pieces]
    out_ref, grads_ref = refs[-2:]
    length = grads_ref.shape[1] // blocks
    block = 0
    for ref in grad_refs:
        for at in range(0, ref.shape[0], pieces * length):
            for piece in range(pieces):
                start = at + piece * length
                grads_ref[piece, block * length : (block + 1) * length] = ref[
                    start : start + length
                ]
            block += 1
    total = jnp.dot(turned_refs[0][...], grads_ref[0], preferred_element_type=jnp.float32)
    for piece in range(1, pieces):
        total += jnp.dot(
            turned_refs[piece][...], grads_ref[piece], preferred_element_type=jnp.float32
        )
    out_ref[...] = total


def outer(grads, turned, blocks, width, half, filled):
    units, count = turned[0].shape
    broad = min(512, width // 2)
    pieces = len(turned)
    steps = width // 2 // broad
    column = lambda i: (0, i + half * steps)
    more = [] if filled is None else [filled]
    return pl.pallas_call(
        functools.partial(outer_kernel, len(grads), pieces, blocks),
        out_shape=jax.ShapeDtypeStruct((units, width), jnp.float32),
        grid=(steps,),
        in_specs=[pl.BlockSpec((g.shape[0], broad), column) for g in grads]
        + [
            pl.BlockSpec((units, count), lambda i: (0, 0), pipeline_mode=pl.Buffered(1))
            for _ in turned
        ]
        + [pl.BlockSpec(memory_space=pl.ANY)] * len(more),
        out_specs=pl.BlockSpec((units, broad), column),
        input_output_aliases={len(grads) + pieces: 0} if more else {},
        scratch_shapes=[pltpu.VMEM((pieces, count, broad), jnp.bfloat16)],
        compiler_params=pltpu.CompilerParams(vmem_limit_bytes=24 << 20),
        cost_estimate=pl.CostEstimate(
            flops=units * count * pieces * width,
            transcendentals=0,
            bytes_accessed=2 * units * width + 2 * count * pieces * width,
        ),
        name="outer",
    )(*grads, *turned, *more)


def attend_kernel(slots, cached, window_free, start, final, *refs):
    place = refs[0]
    q_ref = refs[1]
    keys = refs[2 : 2 + slots]
    values = refs[2 + slots : 2 + 2 * slots]
    at = 2 + 2 * slots
    if not start:
        max_in, sum_in, acc_in = refs[at : at + 3]
        at += 3
    if final:
        out_ref = refs[at]
        at += 1
    else:
        max_out, sum_out, acc_out = refs[at : at + 3]
        at += 3
    scores_ref = refs[at]
    tokens = q_ref.shape[0]
    heads = q_ref.shape[1] // HEAD_SIZE
    count = keys[0].shape[1]
    lanes = 128
    power = math.log2(math.e) / math.sqrt(HEAD_SIZE)
    queries = jnp.concatenate(
        [q_ref[:, j * HEAD_SIZE : (j + 1) * HEAD_SIZE] for j in range(heads)], axis=0
    )
    rows = heads * tokens
    new = count - cached
    gap = lax.broadcasted_iota(jnp.int32, (tokens, new), 1) - lax.broadcasted_iota(
        jnp.int32, (tokens, new), 0
    )
    gap = jnp.concatenate([gap] * heads, axis=0)
    if not window_free:
        gap_cached = lax.broadcasted_iota(jnp.int32, (tokens, cached), 1) - (
            lax.broadcasted_iota(jnp.int32, (tokens, cached), 0)
        )
        gap_cached = jnp.concatenate([gap_cached] * heads, axis=0)
    largest = jnp.full((rows, lanes), HIDDEN, jnp.float32)
    for s in range(slots):
        old = lax.dot_general(
            queries,
            keys[s][0, :cached, :],
            (((1,), (1,)), ((), ())),
            preferred_element_type=jnp.float32,
        )
        if not window_free:
            old = jnp.where(gap_cached > place[slots + s], old, HIDDEN)
        fresh = lax.dot_general(
            queries,
            keys[s][0, cached:, :],
            (((1,), (1,)), ((), ())),
            preferred_element_type=jnp.float32,
        )
        seen = gap <= place[s]
        if not window_free:
            seen = seen & (gap > place[s] - WINDOW)
        fresh = jnp.where(seen, fresh, HIDDEN)
        base = s * count
        scores_ref[:, base : base + cached] = old
        scores_ref[:, base + cached : base + count] = fresh
        for j in range(cached // lanes):
            largest = jnp.maximum(largest, old[:, j * lanes : (j + 1) * lanes])
        for j in range(new // lanes):
            largest = jnp.maximum(largest, fresh[:, j * lanes : (j + 1) * lanes])
    top = jnp.max(largest, axis=1, keepdims=True)
    if not start:
        before = max_in[0][:, :1]
        top = jnp.maximum(top, before)
        rescale = jnp.exp2((before - top) * power)
        total = sum_in[0] * rescale
        acc = acc_in[0] * rescale
    else:
        total = jnp.zeros((rows, lanes), jnp.float32)
        acc = jnp.zeros((rows, HEAD_SIZE), jnp.float32)
    for s in range(slots):
        weights = jnp.exp2((scores_ref[:, s * count : (s + 1) * count] - top) * power)
        for j in range(count // lanes):
            total = total + weights[:, j * lanes : (j + 1) * lanes]
        acc = acc + jnp.dot(
            weights.astype(jnp.bfloat16), values[s][0], preferred_element_type=jnp.float32
        )
    if final:
        result = acc / jnp.sum(total, axis=1, keepdims=True)
        for j in range(heads):
            out_ref[:, j * HEAD_SIZE : (j + 1) * HEAD_SIZE] = result[
                j * tokens : (j + 1) * tokens
            ].astype(jnp.bfloat16)
    else:
        max_out[0] = jnp.broadcast_to(top, (rows, lanes))
        sum_out[0] = total
        acc_out[0] = acc


def attend(queries, blocks, places, cached, window_free, state, final):
    slots = len(blocks)
    tokens = queries.shape[0]
    key_arrays = [b[0] for b in blocks]
    value_arrays = [b[1] for b in blocks]
    heads_kv = key_arrays[0][0].shape[2] // HEAD_SIZE
    group = queries.shape[1] // heads_kv
    count = key_arrays[0][0].shape[1]
    rows = tokens * group // HEAD_SIZE

    def plane_spec(plane):
        return pl.BlockSpec((1, count, HEAD_SIZE), lambda h, place, plane=plane: (plane, 0, h))

    carried = pl.BlockSpec((1, rows, HEAD_SIZE), lambda h, place: (h, 0, 0))
    wide = pl.BlockSpec((tokens, group), lambda h, place: (0, h))
    in_specs = [wide]
    in_specs += [plane_spec(p) for _, p in key_arrays]
    in_specs += [plane_spec(p) for _, p in value_arrays]
    operands = [queries] + [a for a, _ in key_arrays] + [a for a, _ in value_arrays]
    if state is not None:
        in_specs += [carried] * 3
        operands += list(state)
    shape = jax.ShapeDtypeStruct((heads_kv, rows, HEAD_SIZE), jnp.float32)
    if final:
        out_specs, out_shape = wide, jax.ShapeDtypeStruct(queries.shape, jnp.bfloat16)
    else:
        out_specs, out_shape = (carried,) * 3, (shape,) * 3
    work = queries.shape[0] * queries.shape[1] * slots * count
    return pl.pallas_call(
        functools.partial(attend_kernel, slots, cached, window_free, state is None, final),
        out_shape=out_shape,
        grid_spec=pltpu.PrefetchScalarGridSpec(
            num_scalar_prefetch=1,
            grid=(heads_kv,),
            in_specs=in_specs,
            out_specs=out_specs,
            scratch_shapes=[pltpu.VMEM((rows, slots * count), jnp.float32)],
        ),
        cost_estimate=pl.CostEstimate(
            flops=4 * work, transcendentals=work // HEAD_SIZE, bytes_accessed=work // 64
        ),
        name="attend",
    )(places, *operands)


def attention(query, keys_values, cache):
    ctx_size = lax.axis_size("ctx")
    here = lax.axis_index("ctx")
    tokens = query.shape[0]
    cached = cache.shape[1]
    window_free = (cached + tokens) * ctx_size <= WINDOW

    def places(offsets):
        new, old = [], []
        for s in offsets:
            owner = here ^ s
            new.append((here - owner) * tokens)
            old.append(cached * ctx_size + here * tokens - owner * cached - WINDOW)
        return jnp.stack(new + old).astype(jnp.int32)

    stage = functools.partial(attend, query, cached=cached, window_free=window_free)
    own = jnp.concatenate([cache, keys_values], axis=1)
    bits = link_bits()
    if len(bits) != 2:
        held = [(own, 0)]
        for bit in [1] + bits:
            held = held + [(swap(a, bit), s ^ bit) for a, s in held]
        state = None
        for index, (a, s) in enumerate(held):
            last = index == len(held) - 1
            state = stage([((a, 0), (a, 1))], places([s]), state=state, final=last)
        return state
    parity = here % 2
    near = jnp.where(parity == 0, bits[0], bits[1])
    far = jnp.where(parity == 0, bits[1], bits[0])
    blocks = gather(own)
    slots = [((b, 0), (b, 1)) for b in blocks]
    across = near ^ far
    state = stage(slots[:2], places([0, 1]), state=None, final=False)
    state = stage(
        [slots[2], slots[3], slots[5], slots[6]],
        places([near, near ^ 1, far ^ 1, far]),
        state=state,
        final=False,
    )
    return stage(
        [slots[4], slots[7]], places([across, across ^ 1]), state=state, final=True
    )


def planes_of(value, relay):
    blocks = [value]
    for k in range(1, lax.axis_size("exp")):
        source, bits = (blocks[k - 1], 1) if relay and k > 1 and k % 2 else (value, k)
        blocks.append(swap_plane(source, bits))
    return blocks


def on_device(
    query,
    keys_values,
    cache,
    residual,
    out_proj,
    norm_gain,
    router,
    expert_ids,
    w_gate,
    w_up,
    w_down,
    cotangent,
):
    ctx_size = lax.axis_size("ctx")
    planes = lax.axis_size("exp")
    plane = lax.axis_index("exp")
    experts = router.shape[1]
    row_count, width = residual.shape

    tags = jnp.pad(expert_ids.astype(jnp.bfloat16), ((0, 0), (0, HEAD_SIZE - 2)))
    tagged = planes_of(jnp.concatenate([cotangent, tags], axis=1), False)
    grads = gather(jnp.concatenate(tagged, axis=0))
    tall_router = jnp.pad(router, ((0, 0), (0, HEAD_SIZE - experts)))
    query, tall_router = lax.optimization_barrier((query, tall_router))

    attn = attention(query, keys_values, cache)

    place = jnp.full((1,), plane, jnp.int32)
    hidden_one, *shares = project(
        place, attn, pltpu.with_memory_space_constraint(out_proj, pltpu.HBM), residual
    )
    for k in range(0, planes, 2):
        both = swap_plane(shares[k], 1)
        if k:
            both = (shares[k - 1] + both.astype(jnp.float32)).astype(jnp.bfloat16)
            both = swap_plane(both, k)
        hidden_one = hidden_one + both.astype(jnp.float32)
    mean_square = jnp.mean(hidden_one * hidden_one, axis=-1, keepdims=True)
    normed = (hidden_one * lax.rsqrt(mean_square + EPSILON) * norm_gain).astype(jnp.bfloat16)

    in_place = lambda a: pltpu.with_memory_space_constraint(a, pltpu.HBM)
    gate_mat = in_place(w_gate[0])
    up_mat = in_place(w_up[0])
    down_mat = in_place(w_down[0])
    blocks = planes_of(normed, True)
    hidden, turned, counts = [], [], []
    for k in range(0, planes, 2):
        rows = gather(jnp.concatenate(blocks[k : k + 2], axis=0))
        piece = (k, k + 2, (planes * row_count, row_count))
        plain, flipped = rise(place, grads, piece, tall_router, rows, gate_mat, up_mat)
        hidden.append(plain)
        turned.append(flipped)
        counts.append([r.shape[0] for r in rows])
    layer = hidden_one
    for k in range(0, planes, 2):
        parts = fall(hidden[k // 2], down_mat, counts[k // 2])
        summed = scatter(parts)
        both = plus(summed[:row_count], swap_plane(summed[row_count:], 1))
        if k:
            both = swap_plane(both, k)
        layer = layer + both.astype(jnp.float32)
    layer_out = layer.astype(jnp.bfloat16)

    gradient = outer(grads, turned, ctx_size, width, 0, None)
    gradient = outer(grads, turned, ctx_size, width, 1, gradient)
    return (layer_out, gradient[None])


def solution(mesh):
    placed = (
        P("ctx", "exp"),
        P(None, "ctx", "exp"),
        P(None, "ctx", "exp"),
        P(("ctx", "exp"), None),
        P("exp", None),
        P(),
        P(),
        P(("ctx", "exp"), None),
        P("exp", None, "ctx"),
        P("exp", None, "ctx"),
        P("exp", "ctx", None),
        P(("ctx", "exp"), None),
    )

    return jax.shard_map(
        on_device,
        mesh=mesh,
        in_specs=placed,
        out_specs=(P(("ctx", "exp"), None), P("exp", "ctx", None)),
        check_vma=False,
    )
```

```python
import functools
import math

import jax
import jax.numpy as jnp
from jax import lax
from jax.experimental import pallas as pl
from jax.experimental.pallas import tpu as pltpu
from jax.sharding import PartitionSpec as P


HEAD_SIZE = 128
WINDOW = 4096
HIDDEN = -1e30
EPSILON = 1e-05


def swap(value, bit):
    return lax.ppermute(value, "ctx", [(i, i ^ bit) for i in range(lax.axis_size("ctx"))])


def swap_plane(value, bits):
    return lax.ppermute(value, "exp", [(i, i ^ bits) for i in range(lax.axis_size("exp"))])


def link_bits():
    devices = lax.axis_size("ctx")
    return [1 << b for b in range(1, devices.bit_length() - 1)]


def cross(value, turn):
    near, far = link_bits()
    even, odd = (near, far) if turn == 0 else (far, near)
    pairs = [(i, i ^ (odd if i % 2 else even)) for i in range(lax.axis_size("ctx"))]
    return lax.ppermute(value, "ctx", pairs)


def gather(block):
    bits = link_bits()
    if len(bits) != 2:
        held = block
        for bit in bits + [1]:
            held = jnp.concatenate([held, swap(held, bit)], axis=0)
        return [held]
    beside = cross(block, 0)
    mate = swap(block, 1)
    beside_mate = cross(mate, 0)
    opposite = cross(beside, 1)
    return [
        block,
        mate,
        beside,
        beside_mate,
        opposite,
        swap(beside, 1),
        swap(beside_mate, 1),
        swap(opposite, 1),
    ]


def plus(a, b):
    return (a.astype(jnp.float32) + b.astype(jnp.float32)).astype(jnp.bfloat16)


def scatter(parts):
    bits = link_bits()
    if len(bits) != 2:
        held = parts[0]
        for bit in [1] + bits[::-1]:
            middle = held.shape[0] // 2
            held = plus(held[:middle], swap(held[middle:], bit))
        return held
    own, mate, beside, beside_mate, opposite, *theirs = parts
    opposite = plus(opposite, swap(theirs[2], 1))
    returned = cross(opposite, 1)
    beside_mate = plus(beside_mate, swap(theirs[1], 1))
    mate = plus(mate, cross(beside_mate, 0))
    beside = plus(plus(beside, swap(theirs[0], 1)), returned)
    own = plus(own, swap(mate, 1))
    return plus(own, cross(beside, 0))


def widen_kernel(small_ref, wide_ref):
    wide_ref[...] = jnp.zeros_like(wide_ref)
    wide_ref[:, : small_ref.shape[1]] = small_ref[...]


def widen(router):
    return pl.pallas_call(
        widen_kernel,
        out_shape=jax.ShapeDtypeStruct((router.shape[0], HEAD_SIZE), router.dtype),
        name="widen",
    )(router)


def relay_kernel(in_ref, out_ref):
    out_ref[0] = in_ref[0]


def relay(place):
    spec = pl.BlockSpec(memory_space=pltpu.SMEM)
    return pl.pallas_call(
        relay_kernel,
        out_shape=jax.ShapeDtypeStruct(place.shape, place.dtype),
        in_specs=[spec],
        out_specs=spec,
        name="relay",
    )(place)


def rise_kernel(parts, planes, place, router_ref, *refs):
    tag_refs, rows_refs = refs[:parts], refs[parts : 2 * parts]
    gate_ref, up_ref, hidden_ref, turned_ref, rows_all, weight_ref, tags_ref = refs[2 * parts :]

    @pl.when(pl.program_id(0) == 0)
    def _():
        at = 0
        for ref in rows_refs:
            rows_all[at : at + ref.shape[0]] = ref[...]
            at += ref.shape[0]
        first_plane, last_plane, length = planes
        at = 0
        for ref in tag_refs:
            for base in range(0, ref.shape[0], length[0]):
                for k in range(first_plane, last_plane):
                    start = base + k * length[1]
                    tags_ref[at : at + length[1]] = ref[start : start + length[1]]
                    at += length[1]
        logits = jnp.dot(rows_all[...], router_ref[...], preferred_element_type=jnp.float32)
        lane = lax.broadcasted_iota(jnp.int32, logits.shape, 1).astype(jnp.float32)
        tags = tags_ref[...].astype(jnp.float32)
        one, two = tags[:, :1], tags[:, 1:2]
        first = jnp.sum(jnp.where(lane == one, logits, 0.0), axis=1, keepdims=True)
        second = jnp.sum(jnp.where(lane == two, logits, 0.0), axis=1, keepdims=True)
        gate = 1.0 / (1.0 + jnp.exp(second - first))
        mine = place[0].astype(jnp.float32)
        weight = jnp.where(one == mine, gate, 0.0) + jnp.where(two == mine, 1.0 - gate, 0.0)
        weight_ref[...] = jnp.broadcast_to(weight, weight_ref.shape)

    rows = rows_all[...]
    gate = jnp.dot(rows, gate_ref[...], preferred_element_type=jnp.float32)
    up = jnp.dot(rows, up_ref[...], preferred_element_type=jnp.float32)
    hidden = gate / (1.0 + jnp.exp(-gate)) * up * weight_ref[:, :1]
    hidden = hidden.astype(jnp.bfloat16)
    hidden_ref[...] = hidden
    turned_ref[...] = hidden.T


def rise(place, grads, planes, router, rows, gate_mat, up_mat):
    width, units = gate_mat.shape
    tag = lambda g: pl.BlockSpec(
        (g.shape[0], HEAD_SIZE),
        lambda i, place: (0, width // HEAD_SIZE),
        pipeline_mode=pl.Buffered(1),
    )
    count = sum(r.shape[0] for r in rows)
    wide = min(256, units)
    whole = lambda shape: pl.BlockSpec(
        shape, lambda i, place: (0, 0), pipeline_mode=pl.Buffered(1)
    )
    column = lambda i, place: (0, i)
    return pl.pallas_call(
        functools.partial(rise_kernel, len(rows), planes),
        out_shape=[
            jax.ShapeDtypeStruct((count, units), jnp.bfloat16),
            jax.ShapeDtypeStruct((units, count), jnp.bfloat16),
        ],
        grid_spec=pltpu.PrefetchScalarGridSpec(
            num_scalar_prefetch=1,
            grid=(units // wide,),
            in_specs=[whole(router.shape)]
            + [tag(g) for g in grads]
            + [whole(r.shape) for r in rows]
            + [pl.BlockSpec((width, wide), column)] * 2,
            out_specs=[
                pl.BlockSpec((count, wide), column),
                pl.BlockSpec((wide, count), lambda i, place: (i, 0)),
            ],
            scratch_shapes=[
                pltpu.VMEM((count, width), jnp.bfloat16),
                pltpu.VMEM((count, HEAD_SIZE), jnp.float32),
                pltpu.VMEM((count, HEAD_SIZE), jnp.bfloat16),
            ],
        ),
        compiler_params=pltpu.CompilerParams(vmem_limit_bytes=28 << 20),
        cost_estimate=pl.CostEstimate(
            flops=4 * count * width * units,
            transcendentals=count * units,
            bytes_accessed=2 * (2 * width * units + count * width),
        ),
        name="rise",
    )(place, router, *grads, *rows, gate_mat, up_mat)


def fall_kernel(hidden_ref, down_ref, *part_refs):
    part = jnp.dot(hidden_ref[...], down_ref[...], preferred_element_type=jnp.float32)
    part = part.astype(jnp.bfloat16)
    at = 0
    for ref in part_refs:
        ref[...] = part[at : at + ref.shape[0]]
        at += ref.shape[0]


def fall(hidden, down_mat, counts):
    units, width = down_mat.shape
    broad = min(1024, width)
    column = lambda i: (0, i)
    return pl.pallas_call(
        fall_kernel,
        out_shape=[jax.ShapeDtypeStruct((c, width), jnp.bfloat16) for c in counts],
        grid=(width // broad,),
        in_specs=[
            pl.BlockSpec(hidden.shape, lambda i: (0, 0), pipeline_mode=pl.Buffered(1)),
            pl.BlockSpec((units, broad), column),
        ],
        out_specs=[pl.BlockSpec((c, broad), column) for c in counts],
        compiler_params=pltpu.CompilerParams(vmem_limit_bytes=20 << 20),
        cost_estimate=pl.CostEstimate(
            flops=2 * sum(counts) * width * units,
            transcendentals=0,
            bytes_accessed=2 * (width * units + sum(counts) * width),
        ),
        name="fall",
    )(hidden, down_mat)


def project_kernel(planes, place, attn_ref, proj_ref, residual_ref, own_ref, *refs):
    share_refs, sums_ref = refs[:-1], refs[-1]
    rows = own_ref.shape[0]
    sums_ref[...] = jnp.dot(attn_ref[...], proj_ref[...], preferred_element_type=jnp.float32)
    for k in range(planes):
        start = pl.multiple_of((place[0] ^ k) * rows, rows)
        share = sums_ref[pl.ds(start, rows), :]
        if k:
            share_refs[k - 1][...] = share.astype(share_refs[k - 1].dtype)
        else:
            own_ref[...] = share + residual_ref[...].astype(jnp.float32)


def project(place, attn, out_proj, residual):
    rows, width = residual.shape
    tokens = attn.shape[0]
    planes = tokens // rows
    broad = min(1024, width)
    column = lambda i, place: (0, i)
    small = pl.BlockSpec((rows, broad), column)
    return pl.pallas_call(
        functools.partial(project_kernel, planes),
        out_shape=[jax.ShapeDtypeStruct((rows, width), jnp.float32)]
        + [
            jax.ShapeDtypeStruct((rows, width), jnp.bfloat16 if k % 2 else jnp.float32)
            for k in range(1, planes)
        ],
        grid_spec=pltpu.PrefetchScalarGridSpec(
            num_scalar_prefetch=1,
            grid=(width // broad,),
            in_specs=[
                pl.BlockSpec(attn.shape, lambda i, place: (0, 0)),
                pl.BlockSpec((out_proj.shape[0], broad), column),
                small,
            ],
            out_specs=[small] * planes,
            scratch_shapes=[pltpu.VMEM((tokens, broad), jnp.float32)],
        ),
        compiler_params=pltpu.CompilerParams(vmem_limit_bytes=16 << 20),
        cost_estimate=pl.CostEstimate(
            flops=2 * tokens * out_proj.shape[0] * width,
            transcendentals=0,
            bytes_accessed=2 * out_proj.shape[0] * width,
        ),
        name="project",
    )(place, attn, out_proj, residual)


def outer_kernel(parts, pieces, blocks, *refs):
    grad_refs = refs[:parts]
    turned_refs = refs[parts : parts + pieces]
    out_ref, grads_ref = refs[-2:]
    length = grads_ref.shape[1] // blocks
    block = 0
    for ref in grad_refs:
        for at in range(0, ref.shape[0], pieces * length):
            for piece in range(pieces):
                start = at + piece * length
                grads_ref[piece, block * length : (block + 1) * length] = ref[
                    start : start + length
                ]
            block += 1
    total = jnp.dot(turned_refs[0][...], grads_ref[0], preferred_element_type=jnp.float32)
    for piece in range(1, pieces):
        total += jnp.dot(
            turned_refs[piece][...], grads_ref[piece], preferred_element_type=jnp.float32
        )
    out_ref[...] = total


def outer(grads, turned, blocks, width, half, filled):
    units, count = turned[0].shape
    broad = min(512, width // 2)
    pieces = len(turned)
    steps = width // 2 // broad
    column = lambda i: (0, i + half * steps)
    more = [] if filled is None else [filled]
    return pl.pallas_call(
        functools.partial(outer_kernel, len(grads), pieces, blocks),
        out_shape=jax.ShapeDtypeStruct((units, width), jnp.float32),
        grid=(steps,),
        in_specs=[pl.BlockSpec((g.shape[0], broad), column) for g in grads]
        + [
            pl.BlockSpec((units, count), lambda i: (0, 0), pipeline_mode=pl.Buffered(1))
            for _ in turned
        ]
        + [pl.BlockSpec(memory_space=pl.ANY)] * len(more),
        out_specs=pl.BlockSpec((units, broad), column),
        input_output_aliases={len(grads) + pieces: 0} if more else {},
        scratch_shapes=[pltpu.VMEM((pieces, count, broad), jnp.bfloat16)],
        compiler_params=pltpu.CompilerParams(vmem_limit_bytes=24 << 20),
        cost_estimate=pl.CostEstimate(
            flops=units * count * pieces * width,
            transcendentals=0,
            bytes_accessed=2 * units * width + 2 * count * pieces * width,
        ),
        name="outer",
    )(*grads, *turned, *more)


def attend_kernel(slots, cached, window_free, start, final, *refs):
    place = refs[0]
    q_ref = refs[1]
    keys = refs[2 : 2 + slots]
    values = refs[2 + slots : 2 + 2 * slots]
    at = 2 + 2 * slots
    if not start:
        max_in, sum_in, acc_in = refs[at : at + 3]
        at += 3
    if final:
        out_ref = refs[at]
        at += 1
    else:
        max_out, sum_out, acc_out = refs[at : at + 3]
        at += 3
    scores_ref = refs[at]
    tokens = q_ref.shape[0]
    heads = q_ref.shape[1] // HEAD_SIZE
    count = keys[0].shape[1]
    lanes = 128
    power = math.log2(math.e) / math.sqrt(HEAD_SIZE)
    queries = jnp.concatenate(
        [q_ref[:, j * HEAD_SIZE : (j + 1) * HEAD_SIZE] for j in range(heads)], axis=0
    )
    rows = heads * tokens
    new = count - cached
    gap = lax.broadcasted_iota(jnp.int32, (tokens, new), 1) - lax.broadcasted_iota(
        jnp.int32, (tokens, new), 0
    )
    gap = jnp.concatenate([gap] * heads, axis=0)
    if not window_free:
        gap_cached = lax.broadcasted_iota(jnp.int32, (tokens, cached), 1) - (
            lax.broadcasted_iota(jnp.int32, (tokens, cached), 0)
        )
        gap_cached = jnp.concatenate([gap_cached] * heads, axis=0)
    largest = jnp.full((rows, lanes), HIDDEN, jnp.float32)
    for s in range(slots):
        old = lax.dot_general(
            queries,
            keys[s][0, :cached, :],
            (((1,), (1,)), ((), ())),
            preferred_element_type=jnp.float32,
        )
        if not window_free:
            old = jnp.where(gap_cached > place[slots + s], old, HIDDEN)
        fresh = lax.dot_general(
            queries,
            keys[s][0, cached:, :],
            (((1,), (1,)), ((), ())),
            preferred_element_type=jnp.float32,
        )
        seen = gap <= place[s]
        if not window_free:
            seen = seen & (gap > place[s] - WINDOW)
        fresh = jnp.where(seen, fresh, HIDDEN)
        base = s * count
        scores_ref[:, base : base + cached] = old
        scores_ref[:, base + cached : base + count] = fresh
        for j in range(cached // lanes):
            largest = jnp.maximum(largest, old[:, j * lanes : (j + 1) * lanes])
        for j in range(new // lanes):
            largest = jnp.maximum(largest, fresh[:, j * lanes : (j + 1) * lanes])
    top = jnp.max(largest, axis=1, keepdims=True)
    if not start:
        before = max_in[0][:, :1]
        top = jnp.maximum(top, before)
        rescale = jnp.exp2((before - top) * power)
        total = sum_in[0] * rescale
        acc = acc_in[0] * rescale
    else:
        total = jnp.zeros((rows, lanes), jnp.float32)
        acc = jnp.zeros((rows, HEAD_SIZE), jnp.float32)
    for s in range(slots):
        weights = jnp.exp2((scores_ref[:, s * count : (s + 1) * count] - top) * power)
        for j in range(count // lanes):
            total = total + weights[:, j * lanes : (j + 1) * lanes]
        acc = acc + jnp.dot(
            weights.astype(jnp.bfloat16), values[s][0], preferred_element_type=jnp.float32
        )
    if final:
        result = acc / jnp.sum(total, axis=1, keepdims=True)
        for j in range(heads):
            out_ref[:, j * HEAD_SIZE : (j + 1) * HEAD_SIZE] = result[
                j * tokens : (j + 1) * tokens
            ].astype(jnp.bfloat16)
    else:
        max_out[0] = jnp.broadcast_to(top, (rows, lanes))
        sum_out[0] = total
        acc_out[0] = acc


def attend(queries, blocks, places, cached, window_free, state, final):
    slots = len(blocks)
    tokens = queries.shape[0]
    key_arrays = [b[0] for b in blocks]
    value_arrays = [b[1] for b in blocks]
    heads_kv = key_arrays[0][0].shape[2] // HEAD_SIZE
    group = queries.shape[1] // heads_kv
    count = key_arrays[0][0].shape[1]
    rows = tokens * group // HEAD_SIZE

    def plane_spec(plane):
        return pl.BlockSpec((1, count, HEAD_SIZE), lambda h, place, plane=plane: (plane, 0, h))

    carried = pl.BlockSpec((1, rows, HEAD_SIZE), lambda h, place: (h, 0, 0))
    wide = pl.BlockSpec((tokens, group), lambda h, place: (0, h))
    in_specs = [wide]
    in_specs += [plane_spec(p) for _, p in key_arrays]
    in_specs += [plane_spec(p) for _, p in value_arrays]
    operands = [queries] + [a for a, _ in key_arrays] + [a for a, _ in value_arrays]
    if state is not None:
        in_specs += [carried] * 3
        operands += list(state)
    shape = jax.ShapeDtypeStruct((heads_kv, rows, HEAD_SIZE), jnp.float32)
    if final:
        out_specs, out_shape = wide, jax.ShapeDtypeStruct(queries.shape, jnp.bfloat16)
    else:
        out_specs, out_shape = (carried,) * 3, (shape,) * 3
    work = queries.shape[0] * queries.shape[1] * slots * count
    return pl.pallas_call(
        functools.partial(attend_kernel, slots, cached, window_free, state is None, final),
        out_shape=out_shape,
        grid_spec=pltpu.PrefetchScalarGridSpec(
            num_scalar_prefetch=1,
            grid=(heads_kv,),
            in_specs=in_specs,
            out_specs=out_specs,
            scratch_shapes=[pltpu.VMEM((rows, slots * count), jnp.float32)],
        ),
        cost_estimate=pl.CostEstimate(
            flops=4 * work, transcendentals=work // HEAD_SIZE, bytes_accessed=work // 64
        ),
        name="attend",
    )(places, *operands)


def attention(query, keys_values, cache):
    ctx_size = lax.axis_size("ctx")
    here = lax.axis_index("ctx")
    tokens = query.shape[0]
    cached = cache.shape[1]
    window_free = (cached + tokens) * ctx_size <= WINDOW

    def places(offsets):
        new, old = [], []
        for s in offsets:
            owner = here ^ s
            new.append((here - owner) * tokens)
            old.append(cached * ctx_size + here * tokens - owner * cached - WINDOW)
        return jnp.stack(new + old).astype(jnp.int32)

    stage = functools.partial(attend, query, cached=cached, window_free=window_free)
    own = jnp.concatenate([cache, keys_values], axis=1)
    bits = link_bits()
    if len(bits) != 2:
        held = [(own, 0)]
        for bit in [1] + bits:
            held = held + [(swap(a, bit), s ^ bit) for a, s in held]
        state = None
        for index, (a, s) in enumerate(held):
            last = index == len(held) - 1
            state = stage([((a, 0), (a, 1))], places([s]), state=state, final=last)
        return state
    parity = here % 2
    near = jnp.where(parity == 0, bits[0], bits[1])
    far = jnp.where(parity == 0, bits[1], bits[0])
    blocks = gather(own)
    slots = [((b, 0), (b, 1)) for b in blocks]
    across = near ^ far
    state = stage(slots[:2], places([0, 1]), state=None, final=False)
    return stage(
        [slots[2], slots[3], slots[5], slots[6], slots[4], slots[7]],
        places([near, near ^ 1, far ^ 1, far, across, across ^ 1]),
        state=state,
        final=True,
    )


def planes_of(value, relay):
    blocks = [value]
    for k in range(1, lax.axis_size("exp")):
        source, bits = (blocks[k - 1], 1) if relay and k > 1 and k % 2 else (value, k)
        blocks.append(swap_plane(source, bits))
    return blocks


def on_device(
    query,
    keys_values,
    cache,
    residual,
    out_proj,
    norm_gain,
    router,
    expert_ids,
    w_gate,
    w_up,
    w_down,
    cotangent,
):
    ctx_size = lax.axis_size("ctx")
    planes = lax.axis_size("exp")
    plane = lax.axis_index("exp")
    row_count, width = residual.shape

    tags = jnp.pad(expert_ids.astype(jnp.bfloat16), ((0, 0), (0, HEAD_SIZE - 2)))
    tagged = planes_of(jnp.concatenate([cotangent, tags], axis=1), False)
    grads = gather(jnp.concatenate(tagged, axis=0))
    tall_router = widen(router)

    attn = attention(query, keys_values, cache)

    place = jnp.full((1,), plane, jnp.int32)
    hidden_one, *shares = project(
        place, attn, pltpu.with_memory_space_constraint(out_proj, pltpu.HBM), residual
    )
    for k in range(0, planes, 2):
        both = swap_plane(shares[k], 1)
        if k:
            both = (shares[k - 1] + both.astype(jnp.float32)).astype(jnp.bfloat16)
            both = swap_plane(both, k)
        hidden_one = hidden_one + both.astype(jnp.float32)
    mean_square = jnp.mean(hidden_one * hidden_one, axis=-1, keepdims=True)
    normed = (hidden_one * lax.rsqrt(mean_square + EPSILON) * norm_gain).astype(jnp.bfloat16)

    in_place = lambda a: pltpu.with_memory_space_constraint(a, pltpu.HBM)
    gate_mat = in_place(w_gate[0])
    up_mat = in_place(w_up[0])
    down_mat = in_place(w_down[0])
    blocks = planes_of(normed, True)
    place = relay(place)
    hidden, turned, counts = [], [], []
    for k in range(0, planes, 2):
        rows = gather(jnp.concatenate(blocks[k : k + 2], axis=0))
        piece = (k, k + 2, (planes * row_count, row_count))
        plain, flipped = rise(place, grads, piece, tall_router, rows, gate_mat, up_mat)
        hidden.append(plain)
        turned.append(flipped)
        counts.append([r.shape[0] for r in rows])
    layer = hidden_one
    for k in range(0, planes, 2):
        parts = fall(hidden[k // 2], down_mat, counts[k // 2])
        summed = scatter(parts)
        both = plus(summed[:row_count], swap_plane(summed[row_count:], 1))
        if k:
            both = swap_plane(both, k)
        layer = layer + both.astype(jnp.float32)
    layer_out = layer.astype(jnp.bfloat16)

    gradient = outer(grads, turned, ctx_size, width, 0, None)
    gradient = outer(grads, turned, ctx_size, width, 1, gradient)
    return (layer_out, gradient[None])


def solution(mesh):
    placed = (
        P("ctx", "exp"),
        P(None, "ctx", "exp"),
        P(None, "ctx", "exp"),
        P(("ctx", "exp"), None),
        P("exp", None),
        P(),
        P(),
        P(("ctx", "exp"), None),
        P("exp", None, "ctx"),
        P("exp", None, "ctx"),
        P("exp", "ctx", None),
        P(("ctx", "exp"), None),
    )

    return jax.shard_map(
        on_device,
        mesh=mesh,
        in_specs=placed,
        out_specs=(P(("ctx", "exp"), None), P("exp", "ctx", None)),
        check_vma=False,
    )
```

```python
import functools
import math

import jax
import jax.numpy as jnp
from jax import lax
from jax.experimental import pallas as pl
from jax.experimental.pallas import tpu as pltpu
from jax.sharding import PartitionSpec as P


HEAD_SIZE = 128
WINDOW = 4096
HIDDEN = -1e30
EPSILON = 1e-05


def swap(value, bit):
    return lax.ppermute(value, "ctx", [(i, i ^ bit) for i in range(lax.axis_size("ctx"))])


def swap_plane(value, bits):
    return lax.ppermute(value, "exp", [(i, i ^ bits) for i in range(lax.axis_size("exp"))])


def link_bits():
    devices = lax.axis_size("ctx")
    return [1 << b for b in range(1, devices.bit_length() - 1)]


def cross(value, turn):
    near, far = link_bits()
    even, odd = (near, far) if turn == 0 else (far, near)
    pairs = [(i, i ^ (odd if i % 2 else even)) for i in range(lax.axis_size("ctx"))]
    return lax.ppermute(value, "ctx", pairs)


def gather(block):
    bits = link_bits()
    if len(bits) != 2:
        held = block
        for bit in bits + [1]:
            held = jnp.concatenate([held, swap(held, bit)], axis=0)
        return [held]
    beside = cross(block, 0)
    mate = swap(block, 1)
    beside_mate = cross(mate, 0)
    opposite = cross(beside, 1)
    return [
        block,
        mate,
        beside,
        beside_mate,
        opposite,
        swap(beside, 1),
        swap(beside_mate, 1),
        swap(opposite, 1),
    ]


def plus(a, b):
    return (a.astype(jnp.float32) + b.astype(jnp.float32)).astype(jnp.bfloat16)


def scatter(parts):
    bits = link_bits()
    if len(bits) != 2:
        held = parts[0]
        for bit in [1] + bits[::-1]:
            middle = held.shape[0] // 2
            held = plus(held[:middle], swap(held[middle:], bit))
        return held
    own, mate, beside, beside_mate, opposite, *theirs = parts
    opposite = plus(opposite, swap(theirs[2], 1))
    returned = cross(opposite, 1)
    beside_mate = plus(beside_mate, swap(theirs[1], 1))
    mate = plus(mate, cross(beside_mate, 0))
    beside = plus(plus(beside, swap(theirs[0], 1)), returned)
    own = plus(own, swap(mate, 1))
    return plus(own, cross(beside, 0))


def widen_kernel(small_ref, wide_ref):
    wide_ref[...] = jnp.zeros_like(wide_ref)
    wide_ref[: small_ref.shape[0]] = small_ref[...]


def widen(router):
    return pl.pallas_call(
        widen_kernel,
        out_shape=jax.ShapeDtypeStruct((16, router.shape[1]), router.dtype),
        name="widen",
    )(router)


def pack_kernel(cache_ref, new_ref, held_ref):
    cached = cache_ref.shape[1]
    held_ref[:, :cached] = cache_ref[...]
    held_ref[:, cached:] = new_ref[...]


def pack(cache, keys_values):
    count = cache.shape[1] + keys_values.shape[1]
    in_place = lambda a: pltpu.with_memory_space_constraint(a, pltpu.HBM)
    return pl.pallas_call(
        pack_kernel,
        out_shape=jax.ShapeDtypeStruct((2, count, cache.shape[2]), cache.dtype),
        compiler_params=pltpu.CompilerParams(vmem_limit_bytes=8 << 20),
        name="pack",
    )(in_place(cache), in_place(keys_values))


def relay_kernel(in_ref, out_ref):
    out_ref[0] = in_ref[0]


def relay(place):
    spec = pl.BlockSpec(memory_space=pltpu.SMEM)
    return pl.pallas_call(
        relay_kernel,
        out_shape=jax.ShapeDtypeStruct(place.shape, place.dtype),
        in_specs=[spec],
        out_specs=spec,
        name="relay",
    )(place)


def rise_kernel(parts, place, router_ref, *refs):
    rows_refs = refs[:parts]
    gate_ref, up_ref, hidden_ref, turned_ref, rows_all, weight_ref, tags_ref = refs[parts:]
    width = rows_all.shape[1]

    @pl.when(pl.program_id(0) == 0)
    def _():
        at = 0
        for ref in rows_refs:
            rows_all[at : at + ref.shape[0]] = ref[:, :width]
            tags_ref[at : at + ref.shape[0]] = ref[:, width:]
            at += ref.shape[0]
        logits = lax.dot_general(
            rows_all[...],
            router_ref[...],
            (((1,), (1,)), ((), ())),
            preferred_element_type=jnp.float32,
        )
        lane = lax.broadcasted_iota(jnp.int32, logits.shape, 1).astype(jnp.float32)
        tags = tags_ref[...].astype(jnp.float32)
        one, two = tags[:, :1], tags[:, 1:2]
        first = jnp.sum(jnp.where(lane == one, logits, 0.0), axis=1, keepdims=True)
        second = jnp.sum(jnp.where(lane == two, logits, 0.0), axis=1, keepdims=True)
        gate = 1.0 / (1.0 + jnp.exp(second - first))
        mine = place[0].astype(jnp.float32)
        weight = jnp.where(one == mine, gate, 0.0) + jnp.where(two == mine, 1.0 - gate, 0.0)
        weight_ref[...] = jnp.broadcast_to(weight, weight_ref.shape)

    rows = rows_all[...]
    gate = jnp.dot(rows, gate_ref[...], preferred_element_type=jnp.float32)
    up = jnp.dot(rows, up_ref[...], preferred_element_type=jnp.float32)
    hidden = gate / (1.0 + jnp.exp(-gate)) * up * weight_ref[:, :1]
    hidden = hidden.astype(jnp.bfloat16)
    hidden_ref[...] = hidden
    turned_ref[...] = hidden.T


def rise(place, router, rows, gate_mat, up_mat):
    width, units = gate_mat.shape
    count = sum(r.shape[0] for r in rows)
    wide = min(256, units)
    whole = lambda shape: pl.BlockSpec(
        shape, lambda i, place: (0, 0), pipeline_mode=pl.Buffered(1)
    )
    column = lambda i, place: (0, i)
    return pl.pallas_call(
        functools.partial(rise_kernel, len(rows)),
        out_shape=[
            jax.ShapeDtypeStruct((count, units), jnp.bfloat16),
            jax.ShapeDtypeStruct((units, count), jnp.bfloat16),
        ],
        grid_spec=pltpu.PrefetchScalarGridSpec(
            num_scalar_prefetch=1,
            grid=(units // wide,),
            in_specs=[whole(router.shape)]
            + [whole(r.shape) for r in rows]
            + [pl.BlockSpec((width, wide), column)] * 2,
            out_specs=[
                pl.BlockSpec((count, wide), column),
                pl.BlockSpec((wide, count), lambda i, place: (i, 0)),
            ],
            scratch_shapes=[
                pltpu.VMEM((count, width), jnp.bfloat16),
                pltpu.VMEM((count, HEAD_SIZE), jnp.float32),
                pltpu.VMEM((count, HEAD_SIZE), jnp.bfloat16),
            ],
        ),
        compiler_params=pltpu.CompilerParams(vmem_limit_bytes=28 << 20),
        cost_estimate=pl.CostEstimate(
            flops=4 * count * width * units,
            transcendentals=count * units,
            bytes_accessed=2 * (2 * width * units + count * width),
        ),
        name="rise",
    )(place, router, *rows, gate_mat, up_mat)


def fall_kernel(hidden_ref, down_ref, *part_refs):
    part = jnp.dot(hidden_ref[...], down_ref[...], preferred_element_type=jnp.float32)
    part = part.astype(jnp.bfloat16)
    at = 0
    for ref in part_refs:
        ref[...] = part[at : at + ref.shape[0]]
        at += ref.shape[0]


def fall(hidden, down_mat, counts):
    units, width = down_mat.shape
    broad = min(1024, width)
    column = lambda i: (0, i)
    return pl.pallas_call(
        fall_kernel,
        out_shape=[jax.ShapeDtypeStruct((c, width), jnp.bfloat16) for c in counts],
        grid=(width // broad,),
        in_specs=[
            pl.BlockSpec(hidden.shape, lambda i: (0, 0), pipeline_mode=pl.Buffered(1)),
            pl.BlockSpec((units, broad), column),
        ],
        out_specs=[pl.BlockSpec((c, broad), column) for c in counts],
        compiler_params=pltpu.CompilerParams(vmem_limit_bytes=20 << 20),
        cost_estimate=pl.CostEstimate(
            flops=2 * sum(counts) * width * units,
            transcendentals=0,
            bytes_accessed=2 * (width * units + sum(counts) * width),
        ),
        name="fall",
    )(hidden, down_mat)


def project_kernel(planes, place, attn_ref, proj_ref, residual_ref, own_ref, *refs):
    share_refs, sums_ref = refs[:-1], refs[-1]
    rows = own_ref.shape[0]
    sums_ref[...] = jnp.dot(attn_ref[...], proj_ref[...], preferred_element_type=jnp.float32)
    for k in range(planes):
        start = pl.multiple_of((place[0] ^ k) * rows, rows)
        share = sums_ref[pl.ds(start, rows), :]
        if k:
            share_refs[k - 1][...] = share.astype(share_refs[k - 1].dtype)
        else:
            own_ref[...] = share + residual_ref[...].astype(jnp.float32)


def project(place, attn, out_proj, residual):
    rows, width = residual.shape
    tokens = attn.shape[0]
    planes = tokens // rows
    broad = min(1024, width)
    column = lambda i, place: (0, i)
    small = pl.BlockSpec((rows, broad), column)
    return pl.pallas_call(
        functools.partial(project_kernel, planes),
        out_shape=[jax.ShapeDtypeStruct((rows, width), jnp.float32)]
        + [
            jax.ShapeDtypeStruct((rows, width), jnp.bfloat16 if k % 2 else jnp.float32)
            for k in range(1, planes)
        ],
        grid_spec=pltpu.PrefetchScalarGridSpec(
            num_scalar_prefetch=1,
            grid=(width // broad,),
            in_specs=[
                pl.BlockSpec(attn.shape, lambda i, place: (0, 0)),
                pl.BlockSpec((out_proj.shape[0], broad), column),
                small,
            ],
            out_specs=[small] * planes,
            scratch_shapes=[pltpu.VMEM((tokens, broad), jnp.float32)],
        ),
        compiler_params=pltpu.CompilerParams(vmem_limit_bytes=16 << 20),
        cost_estimate=pl.CostEstimate(
            flops=2 * tokens * out_proj.shape[0] * width,
            transcendentals=0,
            bytes_accessed=2 * out_proj.shape[0] * width,
        ),
        name="project",
    )(place, attn, out_proj, residual)


def outer_kernel(parts, pieces, blocks, *refs):
    grad_refs = refs[:parts]
    turned_refs = refs[parts : parts + pieces]
    out_ref, grads_ref = refs[-2:]
    length = grads_ref.shape[1] // blocks
    block = 0
    for ref in grad_refs:
        for at in range(0, ref.shape[0], pieces * length):
            for piece in range(pieces):
                start = at + piece * length
                grads_ref[piece, block * length : (block + 1) * length] = ref[
                    start : start + length
                ]
            block += 1
    total = jnp.dot(turned_refs[0][...], grads_ref[0], preferred_element_type=jnp.float32)
    for piece in range(1, pieces):
        total += jnp.dot(
            turned_refs[piece][...], grads_ref[piece], preferred_element_type=jnp.float32
        )
    out_ref[...] = total


def outer(grads, turned, blocks, width, half, filled):
    units, count = turned[0].shape
    broad = min(512, width // 2)
    pieces = len(turned)
    steps = width // 2 // broad
    column = lambda i: (0, i + half * steps)
    more = [] if filled is None else [filled]
    return pl.pallas_call(
        functools.partial(outer_kernel, len(grads), pieces, blocks),
        out_shape=jax.ShapeDtypeStruct((units, width), jnp.float32),
        grid=(steps,),
        in_specs=[pl.BlockSpec((g.shape[0], broad), column) for g in grads]
        + [
            pl.BlockSpec((units, count), lambda i: (0, 0), pipeline_mode=pl.Buffered(1))
            for _ in turned
        ]
        + [pl.BlockSpec(memory_space=pl.ANY)] * len(more),
        out_specs=pl.BlockSpec((units, broad), column),
        input_output_aliases={len(grads) + pieces: 0} if more else {},
        scratch_shapes=[pltpu.VMEM((pieces, count, broad), jnp.bfloat16)],
        compiler_params=pltpu.CompilerParams(vmem_limit_bytes=24 << 20),
        cost_estimate=pl.CostEstimate(
            flops=units * count * pieces * width,
            transcendentals=0,
            bytes_accessed=2 * units * width + 2 * count * pieces * width,
        ),
        name="outer",
    )(*grads, *turned, *more)


def attend_kernel(slots, cached, window_free, start, final, *refs):
    place = refs[0]
    q_ref = refs[1]
    keys = refs[2 : 2 + slots]
    values = refs[2 + slots : 2 + 2 * slots]
    at = 2 + 2 * slots
    if not start:
        max_in, sum_in, acc_in = refs[at : at + 3]
        at += 3
    if final:
        out_ref = refs[at]
        at += 1
    else:
        max_out, sum_out, acc_out = refs[at : at + 3]
        at += 3
    scores_ref = refs[at]
    tokens = q_ref.shape[0]
    heads = q_ref.shape[1] // HEAD_SIZE
    count = keys[0].shape[1]
    lanes = 128
    power = math.log2(math.e) / math.sqrt(HEAD_SIZE)
    queries = jnp.concatenate(
        [q_ref[:, j * HEAD_SIZE : (j + 1) * HEAD_SIZE] for j in range(heads)], axis=0
    )
    rows = heads * tokens
    new = count - cached
    gap = lax.broadcasted_iota(jnp.int32, (tokens, new), 1) - lax.broadcasted_iota(
        jnp.int32, (tokens, new), 0
    )
    gap = jnp.concatenate([gap] * heads, axis=0)
    if not window_free:
        gap_cached = lax.broadcasted_iota(jnp.int32, (tokens, cached), 1) - (
            lax.broadcasted_iota(jnp.int32, (tokens, cached), 0)
        )
        gap_cached = jnp.concatenate([gap_cached] * heads, axis=0)
    largest = jnp.full((rows, lanes), HIDDEN, jnp.float32)
    for s in range(slots):
        old = lax.dot_general(
            queries,
            keys[s][0, :cached, :],
            (((1,), (1,)), ((), ())),
            preferred_element_type=jnp.float32,
        )
        if not window_free:
            old = jnp.where(gap_cached > place[slots + s], old, HIDDEN)
        fresh = lax.dot_general(
            queries,
            keys[s][0, cached:, :],
            (((1,), (1,)), ((), ())),
            preferred_element_type=jnp.float32,
        )
        seen = gap <= place[s]
        if not window_free:
            seen = seen & (gap > place[s] - WINDOW)
        fresh = jnp.where(seen, fresh, HIDDEN)
        base = s * count
        scores_ref[:, base : base + cached] = old
        scores_ref[:, base + cached : base + count] = fresh
        for j in range(cached // lanes):
            largest = jnp.maximum(largest, old[:, j * lanes : (j + 1) * lanes])
        for j in range(new // lanes):
            largest = jnp.maximum(largest, fresh[:, j * lanes : (j + 1) * lanes])
    top = jnp.max(largest, axis=1, keepdims=True)
    if not start:
        before = max_in[0][:, :1]
        top = jnp.maximum(top, before)
        rescale = jnp.exp2((before - top) * power)
        total = sum_in[0] * rescale
        acc = acc_in[0] * rescale
    else:
        total = jnp.zeros((rows, lanes), jnp.float32)
        acc = jnp.zeros((rows, HEAD_SIZE), jnp.float32)
    for s in range(slots):
        weights = jnp.exp2((scores_ref[:, s * count : (s + 1) * count] - top) * power)
        for j in range(count // lanes):
            total = total + weights[:, j * lanes : (j + 1) * lanes]
        acc = acc + jnp.dot(
            weights.astype(jnp.bfloat16), values[s][0], preferred_element_type=jnp.float32
        )
    if final:
        result = acc / jnp.sum(total, axis=1, keepdims=True)
        for j in range(heads):
            out_ref[:, j * HEAD_SIZE : (j + 1) * HEAD_SIZE] = result[
                j * tokens : (j + 1) * tokens
            ].astype(jnp.bfloat16)
    else:
        max_out[0] = jnp.broadcast_to(top, (rows, lanes))
        sum_out[0] = total
        acc_out[0] = acc


def attend(queries, blocks, places, cached, window_free, state, final):
    slots = len(blocks)
    tokens = queries.shape[0]
    key_arrays = [b[0] for b in blocks]
    value_arrays = [b[1] for b in blocks]
    heads_kv = key_arrays[0][0].shape[2] // HEAD_SIZE
    group = queries.shape[1] // heads_kv
    count = key_arrays[0][0].shape[1]
    rows = tokens * group // HEAD_SIZE

    def plane_spec(plane):
        return pl.BlockSpec((1, count, HEAD_SIZE), lambda h, place, plane=plane: (plane, 0, h))

    carried = pl.BlockSpec((1, rows, HEAD_SIZE), lambda h, place: (h, 0, 0))
    wide = pl.BlockSpec((tokens, group), lambda h, place: (0, h))
    in_specs = [wide]
    in_specs += [plane_spec(p) for _, p in key_arrays]
    in_specs += [plane_spec(p) for _, p in value_arrays]
    operands = [queries] + [a for a, _ in key_arrays] + [a for a, _ in value_arrays]
    if state is not None:
        in_specs += [carried] * 3
        operands += list(state)
    shape = jax.ShapeDtypeStruct((heads_kv, rows, HEAD_SIZE), jnp.float32)
    if final:
        out_specs, out_shape = wide, jax.ShapeDtypeStruct(queries.shape, jnp.bfloat16)
    else:
        out_specs, out_shape = (carried,) * 3, (shape,) * 3
    work = queries.shape[0] * queries.shape[1] * slots * count
    return pl.pallas_call(
        functools.partial(attend_kernel, slots, cached, window_free, state is None, final),
        out_shape=out_shape,
        grid_spec=pltpu.PrefetchScalarGridSpec(
            num_scalar_prefetch=1,
            grid=(heads_kv,),
            in_specs=in_specs,
            out_specs=out_specs,
            scratch_shapes=[pltpu.VMEM((rows, slots * count), jnp.float32)],
        ),
        cost_estimate=pl.CostEstimate(
            flops=4 * work, transcendentals=work // HEAD_SIZE, bytes_accessed=work // 64
        ),
        name="attend",
    )(places, *operands)


def attention(query, keys_values, cache):
    ctx_size = lax.axis_size("ctx")
    here = lax.axis_index("ctx")
    tokens = query.shape[0]
    cached = cache.shape[1]
    window_free = (cached + tokens) * ctx_size <= WINDOW

    def places(offsets):
        new, old = [], []
        for s in offsets:
            owner = here ^ s
            new.append((here - owner) * tokens)
            old.append(cached * ctx_size + here * tokens - owner * cached - WINDOW)
        return jnp.stack(new + old).astype(jnp.int32)

    stage = functools.partial(attend, query, cached=cached, window_free=window_free)
    own = pack(cache, keys_values)
    bits = link_bits()
    if len(bits) != 2:
        held = [(own, 0)]
        for bit in [1] + bits:
            held = held + [(swap(a, bit), s ^ bit) for a, s in held]
        state = None
        for index, (a, s) in enumerate(held):
            last = index == len(held) - 1
            state = stage([((a, 0), (a, 1))], places([s]), state=state, final=last)
        return state
    parity = here % 2
    near = jnp.where(parity == 0, bits[0], bits[1])
    far = jnp.where(parity == 0, bits[1], bits[0])
    blocks = gather(own)
    slots = [((b, 0), (b, 1)) for b in blocks]
    across = near ^ far
    state = stage(slots[:2], places([0, 1]), state=None, final=False)
    return stage(
        [slots[2], slots[3], slots[5], slots[6], slots[4], slots[7]],
        places([near, near ^ 1, far ^ 1, far, across, across ^ 1]),
        state=state,
        final=True,
    )


def planes_of(value, relay):
    blocks = [value]
    for k in range(1, lax.axis_size("exp")):
        source, bits = (blocks[k - 1], 1) if relay and k > 1 and k % 2 else (value, k)
        blocks.append(swap_plane(source, bits))
    return blocks


def on_device(
    query,
    keys_values,
    cache,
    residual,
    out_proj,
    norm_gain,
    router,
    expert_ids,
    w_gate,
    w_up,
    w_down,
    cotangent,
):
    ctx_size = lax.axis_size("ctx")
    planes = lax.axis_size("exp")
    plane = lax.axis_index("exp")
    row_count, width = residual.shape

    grads = gather(jnp.concatenate(planes_of(cotangent, False), axis=0))

    attn = attention(query, keys_values, cache)

    place = jnp.full((1,), plane, jnp.int32)
    marked = relay(place)
    marked = relay(marked)
    hidden_one, *shares = project(
        place, attn, pltpu.with_memory_space_constraint(out_proj, pltpu.HBM), residual
    )
    for k in range(0, planes, 2):
        both = swap_plane(shares[k], 1)
        if k:
            both = (shares[k - 1] + both.astype(jnp.float32)).astype(jnp.bfloat16)
            both = swap_plane(both, k)
        hidden_one = hidden_one + both.astype(jnp.float32)
    mean_square = jnp.mean(hidden_one * hidden_one, axis=-1, keepdims=True)
    normed = (hidden_one * lax.rsqrt(mean_square + EPSILON) * norm_gain).astype(jnp.bfloat16)

    in_place = lambda a: pltpu.with_memory_space_constraint(a, pltpu.HBM)
    gate_mat = in_place(w_gate[0])
    up_mat = in_place(w_up[0])
    down_mat = in_place(w_down[0])
    tags = jnp.pad(expert_ids.astype(jnp.bfloat16), ((0, 0), (0, HEAD_SIZE - 2)))
    blocks = planes_of(jnp.concatenate([normed, tags], axis=1), True)
    tall_router = widen(router.T)
    hidden, turned, counts = [], [], []
    for k in range(0, planes, 2):
        if k == 0 and len(link_bits()) == 2:
            near = zip(gather(blocks[0]), gather(blocks[1]))
            rows = [part for both in near for part in both]
        else:
            rows = gather(jnp.concatenate(blocks[k : k + 2], axis=0))
        plain, flipped = rise(marked, tall_router, rows, gate_mat, up_mat)
        hidden.append(plain)
        turned.append(flipped)
        pieces = 8 if len(link_bits()) == 2 else 1
        counts.append([plain.shape[0] // pieces] * pieces)
    layer = hidden_one
    for k in range(0, planes, 2):
        parts = fall(hidden[k // 2], down_mat, counts[k // 2])
        summed = scatter(parts)
        both = plus(summed[:row_count], swap_plane(summed[row_count:], 1))
        if k:
            both = swap_plane(both, k)
        layer = layer + both.astype(jnp.float32)
    layer_out = layer.astype(jnp.bfloat16)

    gradient = outer(grads, turned, ctx_size, width, 0, None)
    gradient = outer(grads, turned, ctx_size, width, 1, gradient)
    return (layer_out, gradient[None])


def solution(mesh):
    placed = (
        P("ctx", "exp"),
        P(None, "ctx", "exp"),
        P(None, "ctx", "exp"),
        P(("ctx", "exp"), None),
        P("exp", None),
        P(),
        P(),
        P(("ctx", "exp"), None),
        P("exp", None, "ctx"),
        P("exp", None, "ctx"),
        P("exp", "ctx", None),
        P(("ctx", "exp"), None),
    )

    return jax.shard_map(
        on_device,
        mesh=mesh,
        in_specs=placed,
        out_specs=(P(("ctx", "exp"), None), P("exp", "ctx", None)),
        check_vma=False,
    )
```

```python
import functools
import math

import jax
import jax.numpy as jnp
from jax import lax
from jax.experimental import pallas as pl
from jax.experimental.pallas import tpu as pltpu
from jax.sharding import PartitionSpec as P


HEAD_SIZE = 128
WINDOW = 4096
HIDDEN = -1e30
EPSILON = 1e-05


def swap(value, bit):
    return lax.ppermute(value, "ctx", [(i, i ^ bit) for i in range(lax.axis_size("ctx"))])


def swap_plane(value, bits):
    return lax.ppermute(value, "exp", [(i, i ^ bits) for i in range(lax.axis_size("exp"))])


def link_bits():
    devices = lax.axis_size("ctx")
    return [1 << b for b in range(1, devices.bit_length() - 1)]


def cross(value, turn):
    near, far = link_bits()
    even, odd = (near, far) if turn == 0 else (far, near)
    pairs = [(i, i ^ (odd if i % 2 else even)) for i in range(lax.axis_size("ctx"))]
    return lax.ppermute(value, "ctx", pairs)


def gather(block):
    bits = link_bits()
    if len(bits) != 2:
        held = block
        for bit in bits + [1]:
            held = jnp.concatenate([held, swap(held, bit)], axis=0)
        return [held]
    beside = cross(block, 0)
    mate = swap(block, 1)
    beside_mate = cross(mate, 0)
    opposite = cross(beside, 1)
    return [
        block,
        mate,
        beside,
        beside_mate,
        opposite,
        swap(beside, 1),
        swap(beside_mate, 1),
        swap(opposite, 1),
    ]


def plus(a, b):
    return (a.astype(jnp.float32) + b.astype(jnp.float32)).astype(jnp.bfloat16)


def scatter(parts):
    bits = link_bits()
    if len(bits) != 2:
        held = parts[0]
        for bit in [1] + bits[::-1]:
            middle = held.shape[0] // 2
            held = plus(held[:middle], swap(held[middle:], bit))
        return held
    own, mate, beside, beside_mate, opposite, *theirs = parts
    opposite = plus(opposite, swap(theirs[2], 1))
    returned = cross(opposite, 1)
    beside_mate = plus(beside_mate, swap(theirs[1], 1))
    mate = plus(mate, cross(beside_mate, 0))
    beside = plus(plus(beside, swap(theirs[0], 1)), returned)
    own = plus(own, swap(mate, 1))
    return plus(own, cross(beside, 0))


def widen_kernel(small_ref, wide_ref):
    wide_ref[...] = jnp.zeros_like(wide_ref)
    wide_ref[: small_ref.shape[0]] = small_ref[...]


def widen(router):
    return pl.pallas_call(
        widen_kernel,
        out_shape=jax.ShapeDtypeStruct((16, router.shape[1]), router.dtype),
        compiler_params=pltpu.CompilerParams(vmem_limit_bytes=2 << 20),
        name="widen",
    )(router)


def pack_kernel(cache_ref, new_ref, held_ref):
    cached = cache_ref.shape[1]
    held_ref[:, :cached] = cache_ref[...]
    held_ref[:, cached:] = new_ref[...]


def pack(cache, keys_values):
    count = cache.shape[1] + keys_values.shape[1]
    in_place = lambda a: pltpu.with_memory_space_constraint(a, pltpu.HBM)
    return pl.pallas_call(
        pack_kernel,
        out_shape=jax.ShapeDtypeStruct((2, count, cache.shape[2]), cache.dtype),
        compiler_params=pltpu.CompilerParams(vmem_limit_bytes=8 << 20),
        name="pack",
    )(in_place(cache), in_place(keys_values))


def relay_kernel(in_ref, out_ref):
    out_ref[0] = in_ref[0]


def relay(place):
    spec = pl.BlockSpec(memory_space=pltpu.SMEM)
    return pl.pallas_call(
        relay_kernel,
        out_shape=jax.ShapeDtypeStruct(place.shape, place.dtype),
        in_specs=[spec],
        out_specs=spec,
        compiler_params=pltpu.CompilerParams(vmem_limit_bytes=1 << 20),
        name="relay",
    )(place)


def rise_kernel(parts, place, router_ref, *refs):
    rows_refs = refs[:parts]
    gate_ref, up_ref, hidden_ref, turned_ref, rows_all, weight_ref, tags_ref = refs[parts:]
    width = rows_all.shape[1]

    @pl.when(pl.program_id(0) == 0)
    def _():
        at = 0
        for ref in rows_refs:
            rows_all[at : at + ref.shape[0]] = ref[:, :width]
            tags_ref[at : at + ref.shape[0]] = ref[:, width:]
            at += ref.shape[0]
        logits = lax.dot_general(
            rows_all[...],
            router_ref[...],
            (((1,), (1,)), ((), ())),
            preferred_element_type=jnp.float32,
        )
        lane = lax.broadcasted_iota(jnp.int32, logits.shape, 1).astype(jnp.float32)
        tags = tags_ref[...].astype(jnp.float32)
        one, two = tags[:, :1], tags[:, 1:2]
        first = jnp.sum(jnp.where(lane == one, logits, 0.0), axis=1, keepdims=True)
        second = jnp.sum(jnp.where(lane == two, logits, 0.0), axis=1, keepdims=True)
        gate = 1.0 / (1.0 + jnp.exp(second - first))
        mine = place[0].astype(jnp.float32)
        weight = jnp.where(one == mine, gate, 0.0) + jnp.where(two == mine, 1.0 - gate, 0.0)
        weight_ref[...] = jnp.broadcast_to(weight, weight_ref.shape)

    rows = rows_all[...]
    gate = jnp.dot(rows, gate_ref[...], preferred_element_type=jnp.float32)
    up = jnp.dot(rows, up_ref[...], preferred_element_type=jnp.float32)
    hidden = gate / (1.0 + jnp.exp(-gate)) * up * weight_ref[:, :1]
    hidden = hidden.astype(jnp.bfloat16)
    hidden_ref[...] = hidden
    turned_ref[...] = hidden.T


def rise(place, router, rows, gate_mat, up_mat):
    width, units = gate_mat.shape
    count = sum(r.shape[0] for r in rows)
    wide = min(256, units)
    whole = lambda shape: pl.BlockSpec(
        shape, lambda i, place: (0, 0), pipeline_mode=pl.Buffered(1)
    )
    column = lambda i, place: (0, i)
    return pl.pallas_call(
        functools.partial(rise_kernel, len(rows)),
        out_shape=[
            jax.ShapeDtypeStruct((count, units), jnp.bfloat16),
            jax.ShapeDtypeStruct((units, count), jnp.bfloat16),
        ],
        grid_spec=pltpu.PrefetchScalarGridSpec(
            num_scalar_prefetch=1,
            grid=(units // wide,),
            in_specs=[whole(router.shape)]
            + [whole(r.shape) for r in rows]
            + [pl.BlockSpec((width, wide), column)] * 2,
            out_specs=[
                pl.BlockSpec((count, wide), column),
                pl.BlockSpec((wide, count), lambda i, place: (i, 0)),
            ],
            scratch_shapes=[
                pltpu.VMEM((count, width), jnp.bfloat16),
                pltpu.VMEM((count, HEAD_SIZE), jnp.float32),
                pltpu.VMEM((count, HEAD_SIZE), jnp.bfloat16),
            ],
        ),
        compiler_params=pltpu.CompilerParams(vmem_limit_bytes=28 << 20),
        cost_estimate=pl.CostEstimate(
            flops=4 * count * width * units,
            transcendentals=count * units,
            bytes_accessed=2 * (2 * width * units + count * width),
        ),
        name="rise",
    )(place, router, *rows, gate_mat, up_mat)


def fall_kernel(hidden_ref, down_ref, *part_refs):
    part = jnp.dot(hidden_ref[...], down_ref[...], preferred_element_type=jnp.float32)
    part = part.astype(jnp.bfloat16)
    at = 0
    for ref in part_refs:
        ref[...] = part[at : at + ref.shape[0]]
        at += ref.shape[0]


def fall(hidden, down_mat, counts):
    units, width = down_mat.shape
    broad = min(1024, width)
    column = lambda i: (0, i)
    return pl.pallas_call(
        fall_kernel,
        out_shape=[jax.ShapeDtypeStruct((c, width), jnp.bfloat16) for c in counts],
        grid=(width // broad,),
        in_specs=[
            pl.BlockSpec(hidden.shape, lambda i: (0, 0), pipeline_mode=pl.Buffered(1)),
            pl.BlockSpec((units, broad), column),
        ],
        out_specs=[pl.BlockSpec((c, broad), column) for c in counts],
        compiler_params=pltpu.CompilerParams(vmem_limit_bytes=20 << 20),
        cost_estimate=pl.CostEstimate(
            flops=2 * sum(counts) * width * units,
            transcendentals=0,
            bytes_accessed=2 * (width * units + sum(counts) * width),
        ),
        name="fall",
    )(hidden, down_mat)


def project_kernel(planes, place, attn_ref, proj_ref, residual_ref, own_ref, *refs):
    share_refs, sums_ref = refs[:-1], refs[-1]
    rows = own_ref.shape[0]
    sums_ref[...] = jnp.dot(attn_ref[...], proj_ref[...], preferred_element_type=jnp.float32)
    for k in range(planes):
        start = pl.multiple_of((place[0] ^ k) * rows, rows)
        share = sums_ref[pl.ds(start, rows), :]
        if k:
            share_refs[k - 1][...] = share.astype(share_refs[k - 1].dtype)
        else:
            own_ref[...] = share + residual_ref[...].astype(jnp.float32)


def project(place, attn, out_proj, residual):
    rows, width = residual.shape
    tokens = attn.shape[0]
    planes = tokens // rows
    broad = min(1024, width)
    column = lambda i, place: (0, i)
    small = pl.BlockSpec((rows, broad), column)
    return pl.pallas_call(
        functools.partial(project_kernel, planes),
        out_shape=[jax.ShapeDtypeStruct((rows, width), jnp.float32)]
        + [
            jax.ShapeDtypeStruct((rows, width), jnp.bfloat16 if k % 2 else jnp.float32)
            for k in range(1, planes)
        ],
        grid_spec=pltpu.PrefetchScalarGridSpec(
            num_scalar_prefetch=1,
            grid=(width // broad,),
            in_specs=[
                pl.BlockSpec(attn.shape, lambda i, place: (0, 0)),
                pl.BlockSpec((out_proj.shape[0], broad), column),
                small,
            ],
            out_specs=[small] * planes,
            scratch_shapes=[pltpu.VMEM((tokens, broad), jnp.float32)],
        ),
        compiler_params=pltpu.CompilerParams(vmem_limit_bytes=16 << 20),
        cost_estimate=pl.CostEstimate(
            flops=2 * tokens * out_proj.shape[0] * width,
            transcendentals=0,
            bytes_accessed=2 * out_proj.shape[0] * width,
        ),
        name="project",
    )(place, attn, out_proj, residual)


def outer_kernel(parts, pieces, blocks, *refs):
    grad_refs = refs[:parts]
    turned_refs = refs[parts : parts + pieces]
    out_ref, grads_ref = refs[-2:]
    length = grads_ref.shape[1] // blocks
    block = 0
    for ref in grad_refs:
        for at in range(0, ref.shape[0], pieces * length):
            for piece in range(pieces):
                start = at + piece * length
                grads_ref[piece, block * length : (block + 1) * length] = ref[
                    start : start + length
                ]
            block += 1
    total = jnp.dot(turned_refs[0][...], grads_ref[0], preferred_element_type=jnp.float32)
    for piece in range(1, pieces):
        total += jnp.dot(
            turned_refs[piece][...], grads_ref[piece], preferred_element_type=jnp.float32
        )
    out_ref[...] = total


def outer(grads, turned, blocks, width, half, filled):
    units, count = turned[0].shape
    broad = min(512, width // 2)
    pieces = len(turned)
    steps = width // 2 // broad
    column = lambda i: (0, i + half * steps)
    more = [] if filled is None else [filled]
    return pl.pallas_call(
        functools.partial(outer_kernel, len(grads), pieces, blocks),
        out_shape=jax.ShapeDtypeStruct((units, width), jnp.float32),
        grid=(steps,),
        in_specs=[pl.BlockSpec((g.shape[0], broad), column) for g in grads]
        + [
            pl.BlockSpec((units, count), lambda i: (0, 0), pipeline_mode=pl.Buffered(1))
            for _ in turned
        ]
        + [pl.BlockSpec(memory_space=pl.ANY)] * len(more),
        out_specs=pl.BlockSpec((units, broad), column),
        input_output_aliases={len(grads) + pieces: 0} if more else {},
        scratch_shapes=[pltpu.VMEM((pieces, count, broad), jnp.bfloat16)],
        compiler_params=pltpu.CompilerParams(vmem_limit_bytes=24 << 20),
        cost_estimate=pl.CostEstimate(
            flops=units * count * pieces * width,
            transcendentals=0,
            bytes_accessed=2 * units * width + 2 * count * pieces * width,
        ),
        name="outer",
    )(*grads, *turned, *more)


def attend_kernel(slots, cached, window_free, start, final, *refs):
    place = refs[0]
    q_ref = refs[1]
    keys = refs[2 : 2 + slots]
    values = refs[2 + slots : 2 + 2 * slots]
    at = 2 + 2 * slots
    if not start:
        max_in, sum_in, acc_in = refs[at : at + 3]
        at += 3
    if final:
        out_ref = refs[at]
        at += 1
    else:
        max_out, sum_out, acc_out = refs[at : at + 3]
        at += 3
    scores_ref = refs[at]
    tokens = q_ref.shape[0]
    heads = q_ref.shape[1] // HEAD_SIZE
    count = keys[0].shape[1]
    lanes = 128
    power = math.log2(math.e) / math.sqrt(HEAD_SIZE)
    queries = jnp.concatenate(
        [q_ref[:, j * HEAD_SIZE : (j + 1) * HEAD_SIZE] for j in range(heads)], axis=0
    )
    rows = heads * tokens
    new = count - cached
    gap = lax.broadcasted_iota(jnp.int32, (tokens, new), 1) - lax.broadcasted_iota(
        jnp.int32, (tokens, new), 0
    )
    gap = jnp.concatenate([gap] * heads, axis=0)
    if not window_free:
        gap_cached = lax.broadcasted_iota(jnp.int32, (tokens, cached), 1) - (
            lax.broadcasted_iota(jnp.int32, (tokens, cached), 0)
        )
        gap_cached = jnp.concatenate([gap_cached] * heads, axis=0)
    largest = jnp.full((rows, lanes), HIDDEN, jnp.float32)
    for s in range(slots):
        old = lax.dot_general(
            queries,
            keys[s][0, :cached, :],
            (((1,), (1,)), ((), ())),
            preferred_element_type=jnp.float32,
        )
        if not window_free:
            old = jnp.where(gap_cached > place[slots + s], old, HIDDEN)
        fresh = lax.dot_general(
            queries,
            keys[s][0, cached:, :],
            (((1,), (1,)), ((), ())),
            preferred_element_type=jnp.float32,
        )
        seen = gap <= place[s]
        if not window_free:
            seen = seen & (gap > place[s] - WINDOW)
        fresh = jnp.where(seen, fresh, HIDDEN)
        base = s * count
        scores_ref[:, base : base + cached] = old
        scores_ref[:, base + cached : base + count] = fresh
        for j in range(cached // lanes):
            largest = jnp.maximum(largest, old[:, j * lanes : (j + 1) * lanes])
        for j in range(new // lanes):
            largest = jnp.maximum(largest, fresh[:, j * lanes : (j + 1) * lanes])
    top = jnp.max(largest, axis=1, keepdims=True)
    if not start:
        before = max_in[0][:, :1]
        top = jnp.maximum(top, before)
        rescale = jnp.exp2((before - top) * power)
        total = sum_in[0] * rescale
        acc = acc_in[0] * rescale
    else:
        total = jnp.zeros((rows, lanes), jnp.float32)
        acc = jnp.zeros((rows, HEAD_SIZE), jnp.float32)
    for s in range(slots):
        weights = jnp.exp2((scores_ref[:, s * count : (s + 1) * count] - top) * power)
        for j in range(count // lanes):
            total = total + weights[:, j * lanes : (j + 1) * lanes]
        acc = acc + jnp.dot(
            weights.astype(jnp.bfloat16), values[s][0], preferred_element_type=jnp.float32
        )
    if final:
        result = acc / jnp.sum(total, axis=1, keepdims=True)
        for j in range(heads):
            out_ref[:, j * HEAD_SIZE : (j + 1) * HEAD_SIZE] = result[
                j * tokens : (j + 1) * tokens
            ].astype(jnp.bfloat16)
    else:
        max_out[0] = jnp.broadcast_to(top, (rows, lanes))
        sum_out[0] = total
        acc_out[0] = acc


def attend(queries, blocks, places, cached, window_free, state, final):
    slots = len(blocks)
    tokens = queries.shape[0]
    key_arrays = [b[0] for b in blocks]
    value_arrays = [b[1] for b in blocks]
    heads_kv = key_arrays[0][0].shape[2] // HEAD_SIZE
    group = queries.shape[1] // heads_kv
    count = key_arrays[0][0].shape[1]
    rows = tokens * group // HEAD_SIZE

    def plane_spec(plane):
        return pl.BlockSpec((1, count, HEAD_SIZE), lambda h, place, plane=plane: (plane, 0, h))

    carried = pl.BlockSpec((1, rows, HEAD_SIZE), lambda h, place: (h, 0, 0))
    wide = pl.BlockSpec((tokens, group), lambda h, place: (0, h))
    in_specs = [wide]
    in_specs += [plane_spec(p) for _, p in key_arrays]
    in_specs += [plane_spec(p) for _, p in value_arrays]
    operands = [queries] + [a for a, _ in key_arrays] + [a for a, _ in value_arrays]
    if state is not None:
        in_specs += [carried] * 3
        operands += list(state)
    shape = jax.ShapeDtypeStruct((heads_kv, rows, HEAD_SIZE), jnp.float32)
    if final:
        out_specs, out_shape = wide, jax.ShapeDtypeStruct(queries.shape, jnp.bfloat16)
    else:
        out_specs, out_shape = (carried,) * 3, (shape,) * 3
    work = queries.shape[0] * queries.shape[1] * slots * count
    return pl.pallas_call(
        functools.partial(attend_kernel, slots, cached, window_free, state is None, final),
        out_shape=out_shape,
        grid_spec=pltpu.PrefetchScalarGridSpec(
            num_scalar_prefetch=1,
            grid=(heads_kv,),
            in_specs=in_specs,
            out_specs=out_specs,
            scratch_shapes=[pltpu.VMEM((rows, slots * count), jnp.float32)],
        ),
        cost_estimate=pl.CostEstimate(
            flops=4 * work, transcendentals=work // HEAD_SIZE, bytes_accessed=work // 64
        ),
        compiler_params=pltpu.CompilerParams(
            vmem_limit_bytes=4 * rows * slots * count + (10 << 20)
        ),
        name="attend",
    )(places, *operands)


def attention(query, keys_values, cache):
    ctx_size = lax.axis_size("ctx")
    here = lax.axis_index("ctx")
    tokens = query.shape[0]
    cached = cache.shape[1]
    window_free = (cached + tokens) * ctx_size <= WINDOW

    def places(offsets):
        new, old = [], []
        for s in offsets:
            owner = here ^ s
            new.append((here - owner) * tokens)
            old.append(cached * ctx_size + here * tokens - owner * cached - WINDOW)
        return jnp.stack(new + old).astype(jnp.int32)

    stage = functools.partial(attend, query, cached=cached, window_free=window_free)
    own = pack(cache, keys_values)
    bits = link_bits()
    if len(bits) != 2:
        held = [(own, 0)]
        for bit in [1] + bits:
            held = held + [(swap(a, bit), s ^ bit) for a, s in held]
        state = None
        for index, (a, s) in enumerate(held):
            last = index == len(held) - 1
            state = stage([((a, 0), (a, 1))], places([s]), state=state, final=last)
        return state
    parity = here % 2
    near = jnp.where(parity == 0, bits[0], bits[1])
    far = jnp.where(parity == 0, bits[1], bits[0])
    blocks = gather(own)
    slots = [((b, 0), (b, 1)) for b in blocks]
    across = near ^ far
    state = stage(slots[:2], places([0, 1]), state=None, final=False)
    return stage(
        [slots[2], slots[3], slots[5], slots[6], slots[4], slots[7]],
        places([near, near ^ 1, far ^ 1, far, across, across ^ 1]),
        state=state,
        final=True,
    )


def planes_of(value, relay):
    blocks = [value]
    for k in range(1, lax.axis_size("exp")):
        source, bits = (blocks[k - 1], 1) if relay and k > 1 and k % 2 else (value, k)
        blocks.append(swap_plane(source, bits))
    return blocks


def on_device(
    query,
    keys_values,
    cache,
    residual,
    out_proj,
    norm_gain,
    router,
    expert_ids,
    w_gate,
    w_up,
    w_down,
    cotangent,
):
    ctx_size = lax.axis_size("ctx")
    planes = lax.axis_size("exp")
    plane = lax.axis_index("exp")
    row_count, width = residual.shape

    others = planes_of(cotangent, False)[1:]
    in_place = lambda a: pltpu.with_memory_space_constraint(a, pltpu.HBM)
    attn = attention(in_place(query), keys_values, cache)

    place = jnp.full((1,), plane, jnp.int32)
    marked = relay(place)
    marked = relay(marked)
    hidden_one, *shares = project(place, attn, in_place(out_proj), in_place(residual))
    late, hidden_one = lax.optimization_barrier((cotangent, hidden_one))
    grads = gather(jnp.concatenate([late] + others, axis=0))
    for k in range(0, planes, 2):
        both = swap_plane(shares[k], 1)
        if k:
            both = (shares[k - 1] + both.astype(jnp.float32)).astype(jnp.bfloat16)
            both = swap_plane(both, k)
        hidden_one = hidden_one + both.astype(jnp.float32)
    mean_square = jnp.mean(hidden_one * hidden_one, axis=-1, keepdims=True)
    normed = (hidden_one * lax.rsqrt(mean_square + EPSILON) * norm_gain).astype(jnp.bfloat16)

    gate_mat = in_place(w_gate[0])
    up_mat = in_place(w_up[0])
    down_mat = in_place(w_down[0])
    tags = jnp.pad(expert_ids.astype(jnp.bfloat16), ((0, 0), (0, HEAD_SIZE - 2)))
    blocks = planes_of(jnp.concatenate([normed, tags], axis=1), True)
    tall_router = widen(router.T)
    hidden, turned, counts = [], [], []
    for k in range(0, planes, 2):
        if k == 0 and len(link_bits()) == 2:
            near = zip(gather(blocks[0]), gather(blocks[1]))
            rows = [part for both in near for part in both]
        else:
            rows = gather(jnp.concatenate(blocks[k : k + 2], axis=0))
        plain, flipped = rise(marked, tall_router, rows, gate_mat, up_mat)
        hidden.append(plain)
        turned.append(flipped)
        pieces = 8 if len(link_bits()) == 2 else 1
        counts.append([plain.shape[0] // pieces] * pieces)
    layer = hidden_one
    for k in range(0, planes, 2):
        parts = fall(hidden[k // 2], down_mat, counts[k // 2])
        summed = scatter(parts)
        both = plus(summed[:row_count], swap_plane(summed[row_count:], 1))
        if k:
            both = swap_plane(both, k)
        layer = layer + both.astype(jnp.float32)
    layer_out = layer.astype(jnp.bfloat16)

    gradient = outer(grads, turned, ctx_size, width, 0, None)
    gradient = outer(grads, turned, ctx_size, width, 1, gradient)
    return (layer_out, gradient[None])


def solution(mesh):
    placed = (
        P("ctx", "exp"),
        P(None, "ctx", "exp"),
        P(None, "ctx", "exp"),
        P(("ctx", "exp"), None),
        P("exp", None),
        P(),
        P(),
        P(("ctx", "exp"), None),
        P("exp", None, "ctx"),
        P("exp", None, "ctx"),
        P("exp", "ctx", None),
        P(("ctx", "exp"), None),
    )

    return jax.shard_map(
        on_device,
        mesh=mesh,
        in_specs=placed,
        out_specs=(P(("ctx", "exp"), None), P("exp", "ctx", None)),
        check_vma=False,
    )
```

```python
import functools
import math

import jax
import jax.numpy as jnp
from jax import lax
from jax.experimental import pallas as pl
from jax.experimental.pallas import tpu as pltpu
from jax.sharding import PartitionSpec as P


HEAD_SIZE = 128
WINDOW = 4096
HIDDEN = -1e30
EPSILON = 1e-05


def swap(value, bit):
    return lax.ppermute(value, "ctx", [(i, i ^ bit) for i in range(lax.axis_size("ctx"))])


def swap_plane(value, bits):
    return lax.ppermute(value, "exp", [(i, i ^ bits) for i in range(lax.axis_size("exp"))])


def link_bits():
    devices = lax.axis_size("ctx")
    return [1 << b for b in range(1, devices.bit_length() - 1)]


def cross(value, turn):
    near, far = link_bits()
    even, odd = (near, far) if turn == 0 else (far, near)
    pairs = [(i, i ^ (odd if i % 2 else even)) for i in range(lax.axis_size("ctx"))]
    return lax.ppermute(value, "ctx", pairs)


def gather(block):
    bits = link_bits()
    if len(bits) != 2:
        held = block
        for bit in bits + [1]:
            held = jnp.concatenate([held, swap(held, bit)], axis=0)
        return [held]
    beside = cross(block, 0)
    mate = swap(block, 1)
    beside_mate = cross(mate, 0)
    opposite = cross(beside, 1)
    return [
        block,
        mate,
        beside,
        beside_mate,
        opposite,
        swap(beside, 1),
        swap(beside_mate, 1),
        swap(opposite, 1),
    ]


def plus(a, b):
    return (a.astype(jnp.float32) + b.astype(jnp.float32)).astype(jnp.bfloat16)


def scatter(parts):
    bits = link_bits()
    if len(bits) != 2:
        held = parts[0]
        for bit in [1] + bits[::-1]:
            middle = held.shape[0] // 2
            held = plus(held[:middle], swap(held[middle:], bit))
        return held
    own, mate, beside, beside_mate, opposite, *theirs = parts
    opposite = plus(opposite, swap(theirs[2], 1))
    returned = cross(opposite, 1)
    beside_mate = plus(beside_mate, swap(theirs[1], 1))
    mate = plus(mate, cross(beside_mate, 0))
    beside = plus(plus(beside, swap(theirs[0], 1)), returned)
    own = plus(own, swap(mate, 1))
    return plus(own, cross(beside, 0))


def widen_kernel(small_ref, wide_ref):
    wide_ref[...] = jnp.zeros_like(wide_ref)
    wide_ref[: small_ref.shape[0]] = small_ref[...]


def widen(router):
    return pl.pallas_call(
        widen_kernel,
        out_shape=jax.ShapeDtypeStruct((16, router.shape[1]), router.dtype),
        compiler_params=pltpu.CompilerParams(vmem_limit_bytes=2 << 20),
        name="widen",
    )(router)


def pack_kernel(cache_ref, new_ref, held_ref):
    cached = cache_ref.shape[1]
    held_ref[:, :cached] = cache_ref[...]
    held_ref[:, cached:] = new_ref[...]


def pack(cache, keys_values):
    count = cache.shape[1] + keys_values.shape[1]
    in_place = lambda a: pltpu.with_memory_space_constraint(a, pltpu.HBM)
    return pl.pallas_call(
        pack_kernel,
        out_shape=jax.ShapeDtypeStruct((2, count, cache.shape[2]), cache.dtype),
        compiler_params=pltpu.CompilerParams(vmem_limit_bytes=8 << 20),
        name="pack",
    )(in_place(cache), in_place(keys_values))


def relay_kernel(in_ref, out_ref):
    out_ref[0] = in_ref[0]


def relay(place):
    spec = pl.BlockSpec(memory_space=pltpu.SMEM)
    return pl.pallas_call(
        relay_kernel,
        out_shape=jax.ShapeDtypeStruct(place.shape, place.dtype),
        in_specs=[spec],
        out_specs=spec,
        compiler_params=pltpu.CompilerParams(vmem_limit_bytes=1 << 20),
        name="relay",
    )(place)


def rise_kernel(parts, place, router_ref, *refs):
    rows_refs = refs[:parts]
    gate_ref, up_ref, hidden_ref, turned_ref, rows_all, weight_ref, tags_ref = refs[parts:]
    width = rows_all.shape[1]

    @pl.when(pl.program_id(0) == 0)
    def _():
        at = 0
        for ref in rows_refs:
            rows_all[at : at + ref.shape[0]] = ref[:, :width]
            tags_ref[at : at + ref.shape[0]] = ref[:, width:]
            at += ref.shape[0]
        logits = lax.dot_general(
            rows_all[...],
            router_ref[...],
            (((1,), (1,)), ((), ())),
            preferred_element_type=jnp.float32,
        )
        lane = lax.broadcasted_iota(jnp.int32, logits.shape, 1).astype(jnp.float32)
        tags = tags_ref[...].astype(jnp.float32)
        one, two = tags[:, :1], tags[:, 1:2]
        first = jnp.sum(jnp.where(lane == one, logits, 0.0), axis=1, keepdims=True)
        second = jnp.sum(jnp.where(lane == two, logits, 0.0), axis=1, keepdims=True)
        gate = 1.0 / (1.0 + jnp.exp(second - first))
        mine = place[0].astype(jnp.float32)
        weight = jnp.where(one == mine, gate, 0.0) + jnp.where(two == mine, 1.0 - gate, 0.0)
        weight_ref[...] = jnp.broadcast_to(weight, weight_ref.shape)

    rows = rows_all[...]
    gate = jnp.dot(rows, gate_ref[...], preferred_element_type=jnp.float32)
    up = jnp.dot(rows, up_ref[...], preferred_element_type=jnp.float32)
    hidden = gate / (1.0 + jnp.exp(-gate)) * up * weight_ref[:, :1]
    hidden = hidden.astype(jnp.bfloat16)
    hidden_ref[...] = hidden
    turned_ref[...] = hidden.T


def rise(place, router, rows, gate_mat, up_mat):
    width, units = gate_mat.shape
    count = sum(r.shape[0] for r in rows)
    wide = min(256, units)
    whole = lambda shape: pl.BlockSpec(
        shape, lambda i, place: (0, 0), pipeline_mode=pl.Buffered(1)
    )
    column = lambda i, place: (0, i)
    return pl.pallas_call(
        functools.partial(rise_kernel, len(rows)),
        out_shape=[
            jax.ShapeDtypeStruct((count, units), jnp.bfloat16),
            jax.ShapeDtypeStruct((units, count), jnp.bfloat16),
        ],
        grid_spec=pltpu.PrefetchScalarGridSpec(
            num_scalar_prefetch=1,
            grid=(units // wide,),
            in_specs=[whole(router.shape)]
            + [whole(r.shape) for r in rows]
            + [pl.BlockSpec((width, wide), column)] * 2,
            out_specs=[
                pl.BlockSpec((count, wide), column),
                pl.BlockSpec((wide, count), lambda i, place: (i, 0)),
            ],
            scratch_shapes=[
                pltpu.VMEM((count, width), jnp.bfloat16),
                pltpu.VMEM((count, HEAD_SIZE), jnp.float32),
                pltpu.VMEM((count, HEAD_SIZE), jnp.bfloat16),
            ],
        ),
        compiler_params=pltpu.CompilerParams(vmem_limit_bytes=28 << 20),
        cost_estimate=pl.CostEstimate(
            flops=4 * count * width * units,
            transcendentals=count * units,
            bytes_accessed=2 * (2 * width * units + count * width),
        ),
        name="rise",
    )(place, router, *rows, gate_mat, up_mat)


def fall_kernel(hidden_ref, down_ref, *part_refs):
    part = jnp.dot(hidden_ref[...], down_ref[...], preferred_element_type=jnp.float32)
    part = part.astype(jnp.bfloat16)
    at = 0
    for ref in part_refs:
        ref[...] = part[at : at + ref.shape[0]]
        at += ref.shape[0]


def fall(hidden, down_mat, counts, turn):
    units, width = down_mat.shape
    rows = sum(counts)
    broad = min(2048, width)
    column = lambda i: (0, i)
    return pl.pallas_call(
        fall_kernel,
        out_shape=[jax.ShapeDtypeStruct((c, width), jnp.bfloat16) for c in counts],
        grid=(width // broad,),
        in_specs=[
            pl.BlockSpec((rows, units), lambda i: (turn, 0), pipeline_mode=pl.Buffered(1)),
            pl.BlockSpec((units, broad), column),
        ],
        out_specs=[pl.BlockSpec((c, broad), column) for c in counts],
        compiler_params=pltpu.CompilerParams(vmem_limit_bytes=24 << 20),
        cost_estimate=pl.CostEstimate(
            flops=2 * sum(counts) * width * units,
            transcendentals=0,
            bytes_accessed=2 * (width * units + sum(counts) * width),
        ),
        name="fall",
    )(hidden, down_mat)


def project_kernel(planes, place, attn_ref, proj_ref, residual_ref, own_ref, *refs):
    share_refs, sums_ref = refs[:-1], refs[-1]
    rows = own_ref.shape[0]
    sums_ref[...] = jnp.dot(attn_ref[...], proj_ref[...], preferred_element_type=jnp.float32)
    for k in range(planes):
        start = pl.multiple_of((place[0] ^ k) * rows, rows)
        share = sums_ref[pl.ds(start, rows), :]
        if k:
            share_refs[k - 1][...] = share.astype(share_refs[k - 1].dtype)
        else:
            own_ref[...] = share + residual_ref[...].astype(jnp.float32)


def project(place, attn, out_proj, residual):
    rows, width = residual.shape
    tokens = attn.shape[0]
    planes = tokens // rows
    broad = min(1024, width)
    column = lambda i, place: (0, i)
    small = pl.BlockSpec((rows, broad), column)
    return pl.pallas_call(
        functools.partial(project_kernel, planes),
        out_shape=[jax.ShapeDtypeStruct((rows, width), jnp.float32)]
        + [
            jax.ShapeDtypeStruct((rows, width), jnp.bfloat16 if k % 2 else jnp.float32)
            for k in range(1, planes)
        ],
        grid_spec=pltpu.PrefetchScalarGridSpec(
            num_scalar_prefetch=1,
            grid=(width // broad,),
            in_specs=[
                pl.BlockSpec(attn.shape, lambda i, place: (0, 0)),
                pl.BlockSpec((out_proj.shape[0], broad), column),
                small,
            ],
            out_specs=[small] * planes,
            scratch_shapes=[pltpu.VMEM((tokens, broad), jnp.float32)],
        ),
        compiler_params=pltpu.CompilerParams(vmem_limit_bytes=16 << 20),
        cost_estimate=pl.CostEstimate(
            flops=2 * tokens * out_proj.shape[0] * width,
            transcendentals=0,
            bytes_accessed=2 * out_proj.shape[0] * width,
        ),
        name="project",
    )(place, attn, out_proj, residual)


def outer_kernel(parts, pieces, blocks, *refs):
    grad_refs = refs[:parts]
    turned_refs = refs[parts : parts + pieces]
    out_ref, grads_ref = refs[-2:]
    length = grads_ref.shape[1] // blocks
    block = 0
    for ref in grad_refs:
        for at in range(0, ref.shape[0], pieces * length):
            for piece in range(pieces):
                start = at + piece * length
                grads_ref[piece, block * length : (block + 1) * length] = ref[
                    start : start + length
                ]
            block += 1
    total = jnp.dot(turned_refs[0][...], grads_ref[0], preferred_element_type=jnp.float32)
    for piece in range(1, pieces):
        total += jnp.dot(
            turned_refs[piece][...], grads_ref[piece], preferred_element_type=jnp.float32
        )
    out_ref[...] = total


def outer(grads, turned, blocks, width, half, filled):
    units, count = turned[0].shape
    broad = min(512, width // 2)
    pieces = len(turned)
    steps = width // 2 // broad
    column = lambda i: (0, i + half * steps)
    more = [] if filled is None else [filled]
    return pl.pallas_call(
        functools.partial(outer_kernel, len(grads), pieces, blocks),
        out_shape=jax.ShapeDtypeStruct((units, width), jnp.float32),
        grid=(steps,),
        in_specs=[pl.BlockSpec((g.shape[0], broad), column) for g in grads]
        + [
            pl.BlockSpec((units, count), lambda i: (0, 0), pipeline_mode=pl.Buffered(1))
            for _ in turned
        ]
        + [pl.BlockSpec(memory_space=pl.ANY)] * len(more),
        out_specs=pl.BlockSpec((units, broad), column),
        input_output_aliases={len(grads) + pieces: 0} if more else {},
        scratch_shapes=[pltpu.VMEM((pieces, count, broad), jnp.bfloat16)],
        compiler_params=pltpu.CompilerParams(vmem_limit_bytes=24 << 20),
        cost_estimate=pl.CostEstimate(
            flops=units * count * pieces * width,
            transcendentals=0,
            bytes_accessed=2 * units * width + 2 * count * pieces * width,
        ),
        name="outer",
    )(*grads, *turned, *more)


def attend_kernel(slots, cached, window_free, start, final, *refs):
    place = refs[0]
    q_ref = refs[1]
    keys = refs[2 : 2 + slots]
    values = refs[2 + slots : 2 + 2 * slots]
    at = 2 + 2 * slots
    if not start:
        max_in, sum_in, acc_in = refs[at : at + 3]
        at += 3
    if final:
        out_ref = refs[at]
        at += 1
    else:
        max_out, sum_out, acc_out = refs[at : at + 3]
        at += 3
    scores_ref = refs[at]
    tokens = q_ref.shape[0]
    heads = q_ref.shape[1] // HEAD_SIZE
    count = keys[0].shape[1]
    lanes = 128
    power = math.log2(math.e) / math.sqrt(HEAD_SIZE)
    queries = jnp.concatenate(
        [q_ref[:, j * HEAD_SIZE : (j + 1) * HEAD_SIZE] for j in range(heads)], axis=0
    )
    rows = heads * tokens
    new = count - cached
    gap = lax.broadcasted_iota(jnp.int32, (tokens, new), 1) - lax.broadcasted_iota(
        jnp.int32, (tokens, new), 0
    )
    gap = jnp.concatenate([gap] * heads, axis=0)
    if not window_free:
        gap_cached = lax.broadcasted_iota(jnp.int32, (tokens, cached), 1) - (
            lax.broadcasted_iota(jnp.int32, (tokens, cached), 0)
        )
        gap_cached = jnp.concatenate([gap_cached] * heads, axis=0)
    largest = jnp.full((rows, lanes), HIDDEN, jnp.float32)
    for s in range(slots):
        old = lax.dot_general(
            queries,
            keys[s][0, :cached, :],
            (((1,), (1,)), ((), ())),
            preferred_element_type=jnp.float32,
        )
        if not window_free:
            old = jnp.where(gap_cached > place[slots + s], old, HIDDEN)
        fresh = lax.dot_general(
            queries,
            keys[s][0, cached:, :],
            (((1,), (1,)), ((), ())),
            preferred_element_type=jnp.float32,
        )
        seen = gap <= place[s]
        if not window_free:
            seen = seen & (gap > place[s] - WINDOW)
        fresh = jnp.where(seen, fresh, HIDDEN)
        base = s * count
        scores_ref[:, base : base + cached] = old
        scores_ref[:, base + cached : base + count] = fresh
        for j in range(cached // lanes):
            largest = jnp.maximum(largest, old[:, j * lanes : (j + 1) * lanes])
        for j in range(new // lanes):
            largest = jnp.maximum(largest, fresh[:, j * lanes : (j + 1) * lanes])
    top = jnp.max(largest, axis=1, keepdims=True)
    if not start:
        before = max_in[0][:, :1]
        top = jnp.maximum(top, before)
        rescale = jnp.exp2((before - top) * power)
        total = sum_in[0] * rescale
        acc = acc_in[0] * rescale
    else:
        total = jnp.zeros((rows, lanes), jnp.float32)
        acc = jnp.zeros((rows, HEAD_SIZE), jnp.float32)
    for s in range(slots):
        weights = jnp.exp2((scores_ref[:, s * count : (s + 1) * count] - top) * power)
        for j in range(count // lanes):
            total = total + weights[:, j * lanes : (j + 1) * lanes]
        acc = acc + jnp.dot(
            weights.astype(jnp.bfloat16), values[s][0], preferred_element_type=jnp.float32
        )
    if final:
        result = acc / jnp.sum(total, axis=1, keepdims=True)
        for j in range(heads):
            out_ref[:, j * HEAD_SIZE : (j + 1) * HEAD_SIZE] = result[
                j * tokens : (j + 1) * tokens
            ].astype(jnp.bfloat16)
    else:
        max_out[0] = jnp.broadcast_to(top, (rows, lanes))
        sum_out[0] = total
        acc_out[0] = acc


def attend(queries, blocks, places, cached, window_free, state, final):
    slots = len(blocks)
    tokens = queries.shape[0]
    key_arrays = [b[0] for b in blocks]
    value_arrays = [b[1] for b in blocks]
    heads_kv = key_arrays[0][0].shape[2] // HEAD_SIZE
    group = queries.shape[1] // heads_kv
    count = key_arrays[0][0].shape[1]
    rows = tokens * group // HEAD_SIZE

    def plane_spec(plane):
        return pl.BlockSpec((1, count, HEAD_SIZE), lambda h, place, plane=plane: (plane, 0, h))

    carried = pl.BlockSpec((1, rows, HEAD_SIZE), lambda h, place: (h, 0, 0))
    wide = pl.BlockSpec((tokens, group), lambda h, place: (0, h))
    in_specs = [wide]
    in_specs += [plane_spec(p) for _, p in key_arrays]
    in_specs += [plane_spec(p) for _, p in value_arrays]
    operands = [queries] + [a for a, _ in key_arrays] + [a for a, _ in value_arrays]
    if state is not None:
        in_specs += [carried] * 3
        operands += list(state)
    shape = jax.ShapeDtypeStruct((heads_kv, rows, HEAD_SIZE), jnp.float32)
    if final:
        out_specs, out_shape = wide, jax.ShapeDtypeStruct(queries.shape, jnp.bfloat16)
    else:
        out_specs, out_shape = (carried,) * 3, (shape,) * 3
    work = queries.shape[0] * queries.shape[1] * slots * count
    return pl.pallas_call(
        functools.partial(attend_kernel, slots, cached, window_free, state is None, final),
        out_shape=out_shape,
        grid_spec=pltpu.PrefetchScalarGridSpec(
            num_scalar_prefetch=1,
            grid=(heads_kv,),
            in_specs=in_specs,
            out_specs=out_specs,
            scratch_shapes=[pltpu.VMEM((rows, slots * count), jnp.float32)],
        ),
        cost_estimate=pl.CostEstimate(
            flops=4 * work, transcendentals=work // HEAD_SIZE, bytes_accessed=work // 64
        ),
        compiler_params=pltpu.CompilerParams(
            vmem_limit_bytes=4 * rows * slots * count + (10 << 20)
        ),
        name="attend",
    )(places, *operands)


def attention(query, keys_values, cache):
    ctx_size = lax.axis_size("ctx")
    here = lax.axis_index("ctx")
    tokens = query.shape[0]
    cached = cache.shape[1]
    window_free = (cached + tokens) * ctx_size <= WINDOW

    def places(offsets):
        new, old = [], []
        for s in offsets:
            owner = here ^ s
            new.append((here - owner) * tokens)
            old.append(cached * ctx_size + here * tokens - owner * cached - WINDOW)
        return jnp.stack(new + old).astype(jnp.int32)

    stage = functools.partial(attend, query, cached=cached, window_free=window_free)
    own = pack(cache, keys_values)
    bits = link_bits()
    if len(bits) != 2:
        held = [(own, 0)]
        for bit in [1] + bits:
            held = held + [(swap(a, bit), s ^ bit) for a, s in held]
        state = None
        for index, (a, s) in enumerate(held):
            last = index == len(held) - 1
            state = stage([((a, 0), (a, 1))], places([s]), state=state, final=last)
        return state
    parity = here % 2
    near = jnp.where(parity == 0, bits[0], bits[1])
    far = jnp.where(parity == 0, bits[1], bits[0])
    blocks = gather(own)
    slots = [((b, 0), (b, 1)) for b in blocks]
    across = near ^ far
    state = stage(slots[:2], places([0, 1]), state=None, final=False)
    return stage(
        [slots[2], slots[3], slots[5], slots[6], slots[4], slots[7]],
        places([near, near ^ 1, far ^ 1, far, across, across ^ 1]),
        state=state,
        final=True,
    )


def planes_of(value, relay):
    blocks = [value]
    for k in range(1, lax.axis_size("exp")):
        source, bits = (blocks[k - 1], 1) if relay and k > 1 and k % 2 else (value, k)
        blocks.append(swap_plane(source, bits))
    return blocks


def on_device(
    query,
    keys_values,
    cache,
    residual,
    out_proj,
    norm_gain,
    router,
    expert_ids,
    w_gate,
    w_up,
    w_down,
    cotangent,
):
    ctx_size = lax.axis_size("ctx")
    planes = lax.axis_size("exp")
    plane = lax.axis_index("exp")
    row_count, width = residual.shape

    others = planes_of(cotangent, False)[1:]
    in_place = lambda a: pltpu.with_memory_space_constraint(a, pltpu.HBM)
    attn = attention(in_place(query), keys_values, cache)

    place = jnp.full((1,), plane, jnp.int32)
    marked = relay(place)
    marked = relay(marked)
    hidden_one, *shares = project(place, attn, in_place(out_proj), in_place(residual))
    late, hidden_one = lax.optimization_barrier((cotangent, hidden_one))
    grads = gather(jnp.concatenate([late] + others, axis=0))
    for k in range(0, planes, 2):
        both = swap_plane(shares[k], 1)
        if k:
            both = (shares[k - 1] + both.astype(jnp.float32)).astype(jnp.bfloat16)
            both = swap_plane(both, k)
        hidden_one = hidden_one + both.astype(jnp.float32)
    mean_square = jnp.mean(hidden_one * hidden_one, axis=-1, keepdims=True)
    normed = (hidden_one * lax.rsqrt(mean_square + EPSILON) * norm_gain).astype(jnp.bfloat16)

    gate_mat = in_place(w_gate[0])
    up_mat = in_place(w_up[0])
    down_mat = in_place(w_down[0])
    tags = jnp.pad(expert_ids.astype(jnp.bfloat16), ((0, 0), (0, HEAD_SIZE - 2)))
    blocks = planes_of(jnp.concatenate([normed, tags], axis=1), True)
    tall_router = widen(router.T)
    hidden, turned, counts = [], [], []
    for k in range(0, planes, 2):
        if k == 0 and len(link_bits()) == 2:
            near = zip(gather(blocks[0]), gather(blocks[1]))
            rows = [part for both in near for part in both]
        else:
            rows = gather(jnp.concatenate(blocks[k : k + 2], axis=0))
        plain, flipped = rise(marked, tall_router, rows, gate_mat, up_mat)
        hidden.append(plain)
        turned.append(flipped)
        pieces = 8 if len(link_bits()) == 2 else 1
        counts.append([plain.shape[0] // pieces] * pieces)
    layer = hidden_one
    for k in range(0, planes, 2):
        sizes = counts[k // 2]
        if k and len(sizes) == 8:
            leaving = fall(hidden[k // 2], down_mat, sizes[4:], 1)
            parts = fall(hidden[k // 2], down_mat, sizes[:4], 0) + leaving
        else:
            parts = fall(hidden[k // 2], down_mat, sizes, 0)
        summed = scatter(parts)
        both = plus(summed[:row_count], swap_plane(summed[row_count:], 1))
        if k:
            both = swap_plane(both, k)
        layer = layer + both.astype(jnp.float32)
    layer_out = layer.astype(jnp.bfloat16)

    gradient = outer(grads, turned, ctx_size, width, 0, None)
    gradient = outer(grads, turned, ctx_size, width, 1, gradient)
    return (layer_out, gradient[None])


def solution(mesh):
    placed = (
        P("ctx", "exp"),
        P(None, "ctx", "exp"),
        P(None, "ctx", "exp"),
        P(("ctx", "exp"), None),
        P("exp", None),
        P(),
        P(),
        P(("ctx", "exp"), None),
        P("exp", None, "ctx"),
        P("exp", None, "ctx"),
        P("exp", "ctx", None),
        P(("ctx", "exp"), None),
    )

    return jax.shard_map(
        on_device,
        mesh=mesh,
        in_specs=placed,
        out_specs=(P(("ctx", "exp"), None), P("exp", "ctx", None)),
        check_vma=False,
    )
```
